32 devices in a mesh: row: 8 (over y, x, core), col: 4 (over z).
Axes of the slice: x: 2, y: 2, z: 4, core: 2. Of those that a mesh axis runs over, the one named last changes fastest.
Arguments:
- amplitudes: float32 [16, 16, 1024, 1024], P(None, None, 'row', 'col'), may hold values from -6 to 6
- hole_ints: float32 [256, 256], replicated, may hold values from -0.375 to 0.375
- factors: bfloat16 [1024, 1024], replicated, may hold values from -0.1875 to 0.1875
- core_matrix: float32 [1024, 1024], replicated, may hold values from -5 to 5
Outputs:
- residual: float32 [16, 16, 1024, 1024], P(None, None, 'row', 'col')
The draws below stay inside these ranges and needn't reach their ends.
All inputs are finite; a program needn't handle non-finite values.
Results may differ from the reference program's by a relative error of at most 0.0046.
Values sent between devices are 32-bit elements; how exact they have to be, the bound alone decides.
A program may use at most 256 MiB of HBM per device.

```python
import jax
import jax.numpy as jnp
from jax import lax

O = 16
V = 1024
NG = 1024
PAIRS = 256


def steps_of(rng, dims, shards, low, top_value):
    gain = 1.0
    for dim, parts in shards:
        draws = jax.random.uniform(jax.random.fold_in(jax.random.fold_in(rng, 6), dim), (parts,), jnp.float32, low / len(shards), top_value / len(shards))
        gain = gain * jnp.repeat(jnp.exp(draws), dims[dim] // parts).reshape((-1,) + (1,) * (len(dims) - 1 - dim))
    return gain


def centred(rng, shape, deviation, bound, split=(), held_as=jnp.bfloat16):
    factor_of = steps_of(rng, shape, split, -0.22, 0.18) if split else 1.0
    entries = jax.random.normal(rng, shape, jnp.float32) * deviation * factor_of
    return jnp.minimum(jnp.maximum(entries, -bound), bound).astype(held_as)


def setup_inputs(seed: int = 0) -> dict:
    key_of = jax.random.split(jax.random.key(seed), 5)
    return {
        "amplitudes": centred(key_of[0], (O, O, V, V), 1.0, 6.0, ((2, 8), (3, 4)), jnp.float32),
        "hole_ints": centred(key_of[1], (PAIRS, PAIRS), PAIRS ** -0.5, 0.375, (), jnp.float32),
        "factors": centred(key_of[2], (V, NG), V ** -0.5, 0.1875),
        "core_matrix": centred(key_of[3], (NG, NG), 1.0, 5.0, (), jnp.float32),
    }


def particle_ladder(matrix, factors, core_matrix):
    rounded = matrix.astype(jnp.bfloat16)
    left_side = jnp.dot(rounded, factors, preferred_element_type=jnp.float32).astype(jnp.bfloat16)
    inner = jnp.dot(factors.T, left_side, preferred_element_type=jnp.float32)
    weighted = (core_matrix * inner).astype(jnp.bfloat16)
    spread = jnp.dot(factors, weighted, preferred_element_type=jnp.float32).astype(jnp.bfloat16)
    return matrix + jnp.dot(spread, factors.T, preferred_element_type=jnp.float32)


def reference(amplitudes, hole_ints, factors, core_matrix):
    flattened = amplitudes.reshape(PAIRS, V * V)
    hole_term = jnp.dot(hole_ints, flattened, precision=lax.Precision.HIGHEST, preferred_element_type=jnp.float32)
    hole_term = hole_term.reshape(O, O, V, V)
    summed = hole_term + jnp.transpose(hole_term, (1, 0, 3, 2))
    summed = summed.reshape(PAIRS, V, V)
    result = lax.map(lambda matrix: particle_ladder(matrix, factors, core_matrix), summed)
    return result.reshape(O, O, V, V)
```

```python
import functools

import jax
import jax.numpy as jnp
import numpy as np
from jax import lax
from jax.experimental import pallas as pl
from jax.experimental.pallas import tpu as pltpu
from jax.sharding import PartitionSpec as P

VMEM_LIMIT = 60 * 1024 * 1024


def couple_order(occupied):
    listing = []
    for first in range(occupied):
        for second in range(first + 1, occupied):
            listing += [first * occupied + second, second * occupied + first]
    listing += [first * occupied + first for first in range(occupied)]
    return np.array(listing, dtype=np.int32)


def hole_kernel(weights_ref, amplitudes_ref, out_ref):
    weights = weights_ref[...]
    slots = weights.shape[0]
    high = weights.astype(jnp.bfloat16)
    low = (weights - high.astype(jnp.float32)).astype(jnp.bfloat16)
    both = jnp.concatenate([high, low], axis=0)
    by_row = jnp.swapaxes(amplitudes_ref[...], 0, 1)
    terms = []
    for row in range(by_row.shape[0]):
        values = by_row[row]
        top = values.astype(jnp.bfloat16)
        rest = (values - top.astype(jnp.float32)).astype(jnp.bfloat16)
        main = jnp.dot(both, top, preferred_element_type=jnp.float32)
        small = jnp.dot(high, rest, preferred_element_type=jnp.float32)
        terms.append(main[:slots] + (main[slots:] + small))
    out_ref[...] = jnp.swapaxes(jnp.stack(terms, axis=0), 0, 1)


def hole(weights, amplitudes):
    slots, pairs = weights.shape
    _, rows, cols = amplitudes.shape
    step = 8
    return pl.pallas_call(
        hole_kernel,
        grid=(rows // step,),
        in_specs=[
            pl.BlockSpec((slots, pairs), lambda i: (0, 0)),
            pl.BlockSpec((pairs, step, cols), lambda i: (0, i, 0)),
        ],
        out_specs=pl.BlockSpec((slots, step, cols), lambda i: (0, i, 0)),
        out_shape=jax.ShapeDtypeStruct((slots, rows, cols), jnp.float32),
        compiler_params=pltpu.CompilerParams(vmem_limit_bytes=VMEM_LIMIT),
        cost_estimate=pl.CostEstimate(
            flops=6 * slots * pairs * rows * cols,
            bytes_accessed=4 * (slots + pairs) * rows * cols,
            transcendentals=0,
        ),
        name="hole",
    )(weights, amplitudes)


def ladder_kernel(diagonal_ref, blocks_ref, factors_ref, turned_ref, core_ref, out_ref,
                  summed, left, weighted):
    row_count, col_count, _, rows, cols = blocks_ref.shape
    virtual = row_count * rows
    grid_points = factors_ref.shape[1]
    tile = 256
    row_blocks = tile // rows
    col_blocks = tile // cols
    tiles = virtual // tile

    def one(which, _):
        partner = jnp.where(diagonal_ref[0] != 0, which, 1 - which)

        def first(t, _):
            span = pl.ds(pl.multiple_of(t * tile, tile), tile)
            for c in range(tiles):
                straight = jnp.concatenate(
                    [
                        jnp.concatenate(
                            [blocks_ref[t * row_blocks + r, c * col_blocks + q, which] for q in range(col_blocks)],
                            axis=1,
                        )
                        for r in range(row_blocks)
                    ],
                    axis=0,
                )
                other = jnp.concatenate(
                    [
                        jnp.concatenate(
                            [blocks_ref[c * row_blocks + r, t * col_blocks + q, partner] for q in range(col_blocks)],
                            axis=1,
                        )
                        for r in range(row_blocks)
                    ],
                    axis=0,
                )
                summed[span, c * tile:(c + 1) * tile] = straight + other.T
            left[span, :] = jnp.dot(
                summed[span, :].astype(jnp.bfloat16), factors_ref[...], preferred_element_type=jnp.float32
            ).astype(jnp.bfloat16)
            return 0

        lax.fori_loop(0, tiles, first, 0)

        def second(t, _):
            span = pl.ds(pl.multiple_of(t * tile, tile), tile)
            inner = jnp.dot(turned_ref[span, :], left[...], preferred_element_type=jnp.float32)
            weighted[span, :] = (core_ref[span, :] * inner).astype(jnp.bfloat16)
            return 0

        lax.fori_loop(0, grid_points // tile, second, 0)

        def third(t, _):
            span = pl.ds(pl.multiple_of(t * tile, tile), tile)
            spread = jnp.dot(
                factors_ref[span, :], weighted[...], preferred_element_type=jnp.float32
            ).astype(jnp.bfloat16)
            result = summed[span, :] + jnp.dot(spread, turned_ref[...], preferred_element_type=jnp.float32)
            for r in range(row_blocks):
                for c in range(col_count):
                    out_ref[t * row_blocks + r, c, which] = result[r * rows:(r + 1) * rows, c * cols:(c + 1) * cols]
            return 0

        lax.fori_loop(0, tiles, third, 0)
        return 0

    lax.fori_loop(0, 2, one, 0)


def ladder(diagonal, blocks, factors, turned, core_matrix):
    row_count, _, _, rows, _ = blocks.shape
    virtual = row_count * rows
    grid_points = factors.shape[1]
    vmem = pl.BlockSpec(memory_space=pltpu.VMEM)
    return pl.pallas_call(
        ladder_kernel,
        in_specs=[pl.BlockSpec(memory_space=pltpu.SMEM), vmem, vmem, vmem, vmem],
        out_specs=vmem,
        out_shape=jax.ShapeDtypeStruct(blocks.shape, jnp.float32),
        scratch_shapes=[
            pltpu.VMEM((virtual, virtual), jnp.float32),
            pltpu.VMEM((virtual, grid_points), jnp.bfloat16),
            pltpu.VMEM((grid_points, grid_points), jnp.bfloat16),
        ],
        compiler_params=pltpu.CompilerParams(vmem_limit_bytes=VMEM_LIMIT),
        cost_estimate=pl.CostEstimate(
            flops=16 * virtual * virtual * grid_points,
            bytes_accessed=24 * virtual * virtual,
            transcendentals=0,
        ),
        name="ladder",
    )(diagonal, blocks, factors, turned, core_matrix)


def place_kernel(places, group, blocks_ref, *refs):
    out_ref, held, in_sems, out_sems = refs[-4:]
    slots = len(places)

    def fetch(g):
        span = pl.ds(g * group, group)
        return pltpu.make_async_copy(blocks_ref.at[span], held.at[span], in_sems.at[g])

    def put(s):
        return pltpu.make_async_copy(held.at[s], out_ref.at[places[s]], out_sems.at[s])

    for g in range(slots // group):
        fetch(g).start()
    for g in range(slots // group):
        fetch(g).wait()
        for s in range(g * group, (g + 1) * group):
            put(s).start()
    for s in range(slots):
        put(s).wait()


def place(blocks, target, places, pairs):
    slots, rows, cols = blocks.shape
    group = max(1, slots // 8)
    hbm = pl.BlockSpec(memory_space=pl.ANY)
    operands = (blocks,) if target is None else (blocks, target)
    return pl.pallas_call(
        functools.partial(place_kernel, [int(p) for p in places], group),
        in_specs=[hbm] * len(operands),
        out_specs=hbm,
        out_shape=jax.ShapeDtypeStruct((pairs, rows, cols), jnp.float32),
        scratch_shapes=[
            pltpu.VMEM((slots, rows, cols), jnp.float32),
            pltpu.SemaphoreType.DMA((slots // group,)),
            pltpu.SemaphoreType.DMA((slots,)),
        ],
        input_output_aliases={} if target is None else {1: 0},
        compiler_params=pltpu.CompilerParams(vmem_limit_bytes=VMEM_LIMIT),
        cost_estimate=pl.CostEstimate(flops=0, bytes_accessed=8 * slots * rows * cols, transcendentals=0),
        name="place",
    )(*operands)


def exchange(blocks):
    return lax.all_to_all(blocks, ("row", "col"), split_axis=0, concat_axis=0, tiled=True)


MESH = pl.DeviceIdType.MESH


def pairs_of(step, column, slot, occupied):
    odd = occupied - 1
    first = lax.select(column == 0, jnp.int32(odd), lax.rem(step + column, odd))
    second = lax.select(column == 0, step, lax.rem(step + odd - column, odd))
    straight = lax.select(slot == 0, first * occupied + second, second * occupied + first)
    alone = (slot * (occupied // 2) + column) * (occupied + 1)
    return lax.select(step == odd, alone, straight)


def round_robin(occupied):
    odd = occupied - 1
    listing = []
    for step in range(odd):
        for column in range(occupied // 2):
            first = odd if column == 0 else (step + column) % odd
            second = step if column == 0 else (step + odd - column) % odd
            listing += [first * occupied + second, second * occupied + first]
    for column in range(occupied // 2):
        listing += [column * (occupied + 1), (column + occupied // 2) * (occupied + 1)]
    return np.array(listing, dtype=np.int32)


def halves_kernel(weights_ref, amplitudes_ref, factors_hbm, core_hbm,
                  out_ref, slabs_ref, outer_ref, raw_ref, square_ref,
                  tiles, stage, factors, turned, core, core_turned, weighted, weighted_turned,
                  left, summed, held, other, right, right_turned, result, packing, squares,
                  tile_sems, stage_sem, slab_sems, relay_send, relay_recv, raw_send, raw_recv,
                  square_send, square_recv, result_send, kept_sems, out_sems, load_sems):
    row = lax.axis_index("row")
    z = lax.axis_index("col")
    columns = slabs_ref.shape[2] // amplitudes_ref.shape[1]
    pairs, rows, cols = amplitudes_ref.shape
    steps = slabs_ref.shape[0]
    occupied = steps
    virtual = slabs_ref.shape[2]
    half = virtual // 2
    tile = half // 2
    upper = z // 2
    inner = (z == 1) | (z == 2)
    mate = z + 1 - 2 * lax.rem(z, 2)
    across = 3 - z
    own_plane = 1 - upper
    own_rows = pl.multiple_of(upper * half, half)
    far_rows = pl.multiple_of(half - upper * half, half)
    group = stage.shape[0] // (2 * columns)

    barrier = pltpu.get_barrier_semaphore()
    for d in range(1, columns):
        pl.semaphore_signal(barrier, 1, device_id=(lax.rem(row + d, columns), z), device_id_type=MESH)
    for d in range(columns):
        pl.semaphore_signal(barrier, 1, device_id=(d, mate), device_id_type=MESH)

    @pl.when(inner)
    def _():
        pl.semaphore_signal(barrier, 1, device_id=(row, across), device_id_type=MESH)
        pl.semaphore_wait(barrier, 2 * columns)

    @pl.when(jnp.logical_not(inner))
    def _():
        pl.semaphore_wait(barrier, 2 * columns - 1)

    def fetch(b, slot):
        return pltpu.make_async_copy(
            amplitudes_ref.at[:, pl.ds(pl.multiple_of(b * 8, 8), 8), :], tiles.at[slot], tile_sems.at[slot]
        )

    def sent_stage():
        part = stage.at[pl.ds(0, 2 * group * (columns - 1))]
        return pltpu.make_async_copy(part, part, stage_sem)

    def hole_group(g):
        fetch(0, 0).start()

        @pl.when(g > 0)
        def _():
            sent_stage().wait()

        weights = weights_ref[pl.ds(pl.multiple_of(g * stage.shape[0], stage.shape[0]), stage.shape[0]), :]
        slots = weights.shape[0]
        high = weights.astype(jnp.bfloat16)
        low = (weights - high.astype(jnp.float32)).astype(jnp.bfloat16)
        both = jnp.concatenate([high, low], axis=0)
        blocks = rows // 8

        def block(b, _):
            slot = lax.rem(b, 2)

            @pl.when(b + 1 < blocks)
            def _():
                fetch(b + 1, 1 - slot).start()

            fetch(b, slot).wait()
            by_row = jnp.swapaxes(tiles[slot], 0, 1)
            terms = []
            for n in range(8):
                values = by_row[n]
                top = values.astype(jnp.bfloat16)
                rest = (values - top.astype(jnp.float32)).astype(jnp.bfloat16)
                main = jnp.dot(both, top, preferred_element_type=jnp.float32)
                small = jnp.dot(high, rest, preferred_element_type=jnp.float32)
                terms.append(main[:slots] + (main[slots:] + small))
            stage[:, pl.ds(pl.multiple_of(b * 8, 8), 8), :] = jnp.swapaxes(jnp.stack(terms, axis=0), 0, 1)
            return 0

        lax.fori_loop(0, blocks, block, 0)

        def send(n, _):
            step = g * group + n
            place_rows = pl.ds(pl.multiple_of(row * rows, rows), rows)
            for d in range(1, columns):
                to = lax.rem(row + d, columns)
                pltpu.make_async_remote_copy(
                    src_ref=stage.at[pl.ds((n * columns + to) * 2, 2)],
                    dst_ref=slabs_ref.at[step, :, place_rows, :],
                    send_sem=stage_sem,
                    recv_sem=slab_sems.at[step],
                    device_id=(to, z),
                    device_id_type=MESH,
                ).start()
            pltpu.make_async_copy(
                stage.at[pl.ds((n * columns + row) * 2, 2)], slabs_ref.at[step, :, place_rows, :], slab_sems.at[step]
            ).start()
            return 0

        lax.fori_loop(0, group, send, 0)

    def wait_slab(step):
        pltpu.make_async_copy(slabs_ref.at[step], slabs_ref.at[step], slab_sems.at[step]).wait()

    def relay(step):
        return pltpu.make_async_remote_copy(
            src_ref=slabs_ref.at[step], dst_ref=outer_ref.at[step],
            send_sem=relay_send.at[step], recv_sem=relay_recv.at[step],
            device_id=(row, mate), device_id_type=MESH,
        )

    def raw(source, step, plane):
        return pltpu.make_async_remote_copy(
            src_ref=source.at[step, :, pl.ds(far_rows, half), :], dst_ref=raw_ref.at[step, plane],
            send_sem=raw_send.at[2 * step + plane], recv_sem=raw_recv.at[2 * step + plane],
            device_id=(row, across), device_id_type=MESH,
        )

    def square(item):
        slot = lax.rem(item, 2)
        return pltpu.make_async_remote_copy(
            src_ref=squares.at[slot], dst_ref=square_ref.at[item],
            send_sem=square_send.at[slot], recv_sem=square_recv.at[item],
            device_id=(row, across), device_id_type=MESH,
        )

    def item_of(item):
        alone = item >= steps - 1
        step = jnp.minimum(item, steps - 1)
        straight = lax.select(alone, item - (steps - 1), jnp.int32(0))
        flipped = lax.select(alone, item - (steps - 1), jnp.int32(1))
        return alone, step, straight, flipped

    def raw_own(step):
        wait_slab(step)
        raw(slabs_ref, step, own_plane).start()

    def pack(item):
        alone, step, straight, flipped = item_of(item)

        @pl.when(item < steps)
        def _():
            relay(step).wait_recv()
            raw(outer_ref, step, 1 - own_plane).start()

        mine = pltpu.make_async_copy(
            slabs_ref.at[step, :, pl.ds(own_rows, half), :], packing.at[own_plane], load_sems.at[0])
        theirs = pltpu.make_async_copy(
            outer_ref.at[step, :, pl.ds(own_rows, half), :], packing.at[1 - own_plane], load_sems.at[1])
        mine.start()
        theirs.start()

        @pl.when(item >= 2)
        def _():
            square(item).wait_send()

        mine.wait()
        theirs.wait()
        slot = lax.rem(item, 2)
        for a in range(2):
            for b in range(2):
                squares[slot, a * tile:(a + 1) * tile, b * tile:(b + 1) * tile] = (
                    packing[b, straight, a * tile:(a + 1) * tile, :]
                    + packing[a, flipped, b * tile:(b + 1) * tile, :].T
                )
        square(item).start()

    def prepare():
        top = pltpu.make_async_copy(
            factors_hbm.at[pl.ds(own_rows, half), :], factors.at[pl.ds(0, half), :], load_sems.at[0])
        bottom = pltpu.make_async_copy(
            factors_hbm.at[pl.ds(far_rows, half), :], factors.at[pl.ds(half, half), :], load_sems.at[1])
        whole = pltpu.make_async_copy(core_hbm, core, load_sems.at[2])
        for copy in (top, bottom, whole):
            copy.start()
        for copy in (top, bottom, whole):
            copy.wait()

        def turn(t, _):
            span = pl.ds(pl.multiple_of(t * tile, tile), tile)
            for c in range(virtual // tile):
                turned[c * tile:(c + 1) * tile, span] = factors[span, c * tile:(c + 1) * tile].T
                core_turned[c * tile:(c + 1) * tile, span] = core[span, c * tile:(c + 1) * tile].T
            return 0

        lax.fori_loop(0, virtual // tile, turn, 0)

    def kept_result(slot, pair):
        return pltpu.make_async_copy(
            result.at[slot, own_plane * columns + lax.rem(row + upper * (columns // 2), columns)],
            out_ref.at[pair], kept_sems.at[slot])

    def sent_result(slot):
        part = result.at[slot, pl.ds(0, 2 * columns - 1)]
        pltpu.make_async_copy(part, part, result_send.at[slot]).wait()
        kept_result(slot, 0).wait()

    def give(item_step, slot):
        pair = pairs_of(item_step, row, slot, occupied)

        def send(q, _):
            to = lax.rem(q + upper * (columns // 2), columns)
            for p in range(2):
                where = lax.select(own_plane == p, z, mate)

                @pl.when((own_plane != p) | (to != row))
                def _():
                    pltpu.make_async_remote_copy(
                        src_ref=result.at[slot, p * columns + q], dst_ref=out_ref.at[pair],
                        send_sem=result_send.at[slot], recv_sem=out_sems.at[item_step],
                        device_id=(to, where), device_id_type=MESH,
                    ).start()
            return 0

        lax.fori_loop(0, columns, send, 0)
        kept_result(slot, pair).start()

    def ladder_item(item):
        alone, step, straight, flipped = item_of(item)
        loads = [
            pltpu.make_async_copy(
                slabs_ref.at[step, :, pl.ds(own_rows, half), :], held.at[own_plane, :, pl.ds(0, half), :],
                load_sems.at[0]),
            pltpu.make_async_copy(
                slabs_ref.at[step, :, pl.ds(far_rows, half), :], held.at[own_plane, :, pl.ds(half, half), :],
                load_sems.at[1]),
            pltpu.make_async_copy(
                outer_ref.at[step, :, pl.ds(own_rows, half), :], held.at[1 - own_plane, :, pl.ds(0, half), :],
                load_sems.at[2]),
            pltpu.make_async_copy(
                outer_ref.at[step, :, pl.ds(far_rows, half), :], held.at[1 - own_plane, :, pl.ds(half, half), :],
                load_sems.at[3]),
        ]
        late = [
            pltpu.make_async_copy(raw_ref.at[step], other, load_sems.at[4]),
            pltpu.make_async_copy(square_ref.at[item], summed.at[pl.ds(half, half), pl.ds(half, half)],
                                  load_sems.at[5]),
        ]
        for copy in loads:
            copy.start()

        @pl.when(item < steps)
        def _():
            raw(slabs_ref, step, 0).wait_recv()
            raw(slabs_ref, step, 1).wait_recv()

        late[0].start()
        square(item).wait_recv()
        late[1].start()
        for copy in loads + late:
            copy.wait()
        for a in range(2):
            for b in range(2):
                here = slice(a * tile, (a + 1) * tile)
                there = slice(half + b * tile, half + (b + 1) * tile)
                summed[here, b * tile:(b + 1) * tile] = (
                    held[b, straight, here, :] + held[a, flipped, b * tile:(b + 1) * tile, :].T)
                summed[here, there] = other[b, straight, here, :] + held[a, flipped, there, :].T
                summed[there, here] = held[a, straight, there, :] + other[b, flipped, here, :].T

        def first(t, _):
            span = pl.ds(pl.multiple_of(t * tile, tile), tile)
            left[span, :] = jnp.dot(
                summed[span, :].astype(jnp.bfloat16), factors[...], preferred_element_type=jnp.float32
            ).astype(jnp.bfloat16)
            return 0

        lax.fori_loop(0, virtual // tile, first, 0)

        def second(t, _):
            span = pl.ds(pl.multiple_of(t * tile, tile), tile)
            product = jnp.dot(turned[span, :], left[...], preferred_element_type=jnp.float32)
            weighted[span, :] = (core[span, :] * product).astype(jnp.bfloat16)
            weighted_turned[span, :] = (core_turned[span, :] * product).astype(jnp.bfloat16)
            return 0

        lax.fori_loop(0, virtual // tile, second, 0)

        def third(t, _):
            span = pl.ds(pl.multiple_of(t * tile, tile), tile)
            right[span, :] = jnp.dot(
                weighted[span, :], turned[:, 0:half], preferred_element_type=jnp.float32
            ).astype(jnp.bfloat16)
            return 0

        lax.fori_loop(0, virtual // tile, third, 0)

        @pl.when((item > 0) & (item <= steps - 1))
        def _():
            sent_result(0)

        @pl.when(((item > 0) & (item < steps - 1)) | (item == steps))
        def _():
            sent_result(1)

        per = tile // rows

        def fourth(t, _):
            span = pl.ds(pl.multiple_of(t * tile, tile), tile)
            value = summed[span, 0:half] + jnp.dot(
                factors[span, :], right[...], preferred_element_type=jnp.float32)
            for p in range(2):
                for n in range(per):
                    result[straight, p * columns + t * per + n] = (
                        value[n * rows:(n + 1) * rows, p * tile:(p + 1) * tile])
            return 0

        lax.fori_loop(0, virtual // tile, fourth, 0)
        give(step, straight)

        @pl.when(jnp.logical_not(alone))
        def _():
            for b in range(2):
                right_turned[b * tile:(b + 1) * tile, :] = jnp.dot(
                    factors[b * tile:(b + 1) * tile, :], weighted_turned[...], preferred_element_type=jnp.float32
                ).astype(jnp.bfloat16)

            def fifth(t, _):
                span = pl.ds(pl.multiple_of(t * tile, tile), tile)
                for p in range(2):
                    value = summed[p * tile:(p + 1) * tile, span] + jnp.dot(
                        right_turned[p * tile:(p + 1) * tile, :], turned[:, span],
                        preferred_element_type=jnp.float32)
                    value = value.T
                    for n in range(per):
                        result[1, p * columns + t * per + n] = value[n * rows:(n + 1) * rows, :]
                return 0

            lax.fori_loop(0, virtual // tile, fifth, 0)
            give(step, 1)

    groups = steps // group

    @pl.when(jnp.logical_not(inner))
    def _():
        def outer_group(g, _):
            hole_group(g)
            for n in range(group):
                wait_slab(g * group + n)
                relay(g * group + n).start()
            return 0

        lax.fori_loop(0, groups, outer_group, 0)

        def finish(step, _):
            relay(step).wait_send()
            return 0

        lax.fori_loop(0, steps, finish, 0)

    @pl.when(inner)
    def _():
        hole_group(0)
        prepare()
        raw_own(0)
        raw_own(1)
        pack(0)

        def body(item, _):
            @pl.when((lax.rem(item, group) == 0) & (item < steps - group))
            def _():
                hole_group(item // group + 1)

            @pl.when(item < steps)
            def _():
                pack(item + 1)

            ladder_item(item)

            @pl.when(item + 2 < steps)
            def _():
                raw_own(item + 2)

            return 0

        lax.fori_loop(0, steps + 1, body, 0)

        def finish(n, _):
            raw(slabs_ref, n // 2, lax.rem(n, 2)).wait_send()
            return 0

        lax.fori_loop(0, 2 * steps, finish, 0)
        square(steps - 1).wait_send()
        square(steps).wait_send()
        sent_result(0)
        sent_result(1)

    sent_stage().wait()

    def arrived(tiles_of_step):
        def wait(step, _):
            part = out_ref.at[pl.ds(0, tiles_of_step)]
            pltpu.make_async_copy(part, part, out_sems.at[step]).wait()
            return 0

        lax.fori_loop(0, steps, wait, 0)

    @pl.when(inner)
    def _():
        arrived(2 * (columns - 1))

    @pl.when(jnp.logical_not(inner))
    def _():
        arrived(2 * columns)


def halves(amplitudes, hole_ints, factors, core_matrix, columns):
    occupied, _, rows, cols = amplitudes.shape
    pairs = occupied * occupied
    virtual = factors.shape[0]
    grid_points = factors.shape[1]
    steps = occupied
    half = virtual // 2
    tile = half // 2
    group = 2
    f32, bf16 = jnp.float32, jnp.bfloat16
    hbm = pl.BlockSpec(memory_space=pl.ANY)
    vmem = pl.BlockSpec(memory_space=pltpu.VMEM)
    dma = pltpu.SemaphoreType.DMA
    weights = jnp.take(hole_ints, jnp.asarray(round_robin(occupied)), axis=0)
    outs = pl.pallas_call(
        halves_kernel,
        in_specs=[vmem, hbm, hbm, hbm],
        out_specs=[hbm] * 5,
        out_shape=[
            jax.ShapeDtypeStruct((pairs, rows, cols), f32),
            jax.ShapeDtypeStruct((steps, 2, virtual, cols), f32),
            jax.ShapeDtypeStruct((steps, 2, virtual, cols), f32),
            jax.ShapeDtypeStruct((steps, 2, 2, half, cols), f32),
            jax.ShapeDtypeStruct((steps + 1, half, half), f32),
        ],
        scratch_shapes=[
            pltpu.VMEM((2, pairs, 8, cols), f32),
            pltpu.VMEM((group * 2 * columns, rows, cols), f32),
            pltpu.VMEM((virtual, grid_points), bf16),
            pltpu.VMEM((grid_points, virtual), bf16),
            pltpu.VMEM((grid_points, grid_points), f32),
            pltpu.VMEM((grid_points, grid_points), f32),
            pltpu.VMEM((grid_points, grid_points), bf16),
            pltpu.VMEM((grid_points, grid_points), bf16),
            pltpu.VMEM((virtual, grid_points), bf16),
            pltpu.VMEM((virtual, virtual), f32),
            pltpu.VMEM((2, 2, virtual, cols), f32),
            pltpu.VMEM((2, 2, half, cols), f32),
            pltpu.VMEM((grid_points, half), bf16),
            pltpu.VMEM((half, grid_points), bf16),
            pltpu.VMEM((2, 2 * columns, rows, cols), f32),
            pltpu.VMEM((2, 2, half, cols), f32),
            pltpu.VMEM((2, half, half), f32),
            dma((2,)),
            dma,
            dma((steps,)),
            dma((steps,)),
            dma((steps,)),
            dma((2 * steps,)),
            dma((2 * steps,)),
            dma((2,)),
            dma((steps + 1,)),
            dma((2,)),
            dma((2,)),
            dma((steps,)),
            dma((6,)),
        ],
        compiler_params=pltpu.CompilerParams(
            vmem_limit_bytes=VMEM_LIMIT, collective_id=0, has_side_effects=True),
        name="halves",
    )(weights, amplitudes.reshape(pairs, rows, cols), factors, core_matrix)
    return outs[0].reshape(amplitudes.shape)


def local(amplitudes, hole_ints, factors, core_matrix):
    row_count = lax.axis_size("row")
    col_count = lax.axis_size("col")
    devices = row_count * col_count
    occupied, _, rows, cols = amplitudes.shape
    if (row_count, col_count, occupied, rows, cols) == (8, 4, 16, 128, 256):
        return halves(amplitudes, hole_ints, factors, core_matrix, row_count)
    pairs = occupied * occupied
    chunks = pairs // (2 * devices)
    slots = 2 * devices
    flattened = amplitudes.reshape(pairs, rows, cols)
    order = couple_order(occupied)
    weights = jnp.take(hole_ints, jnp.asarray(order), axis=0)
    turned = factors.T
    me = lax.axis_index(("row", "col"))
    first_diagonal = occupied * (occupied - 1) // 2

    arrived = []
    for k in range(chunks):
        term = hole(weights[k * slots:(k + 1) * slots], flattened)
        arrived.append(exchange(term.reshape(devices, 2, rows, cols)))
    returned = []
    for k in range(chunks):
        blocks = arrived[k].reshape(row_count, col_count, 2, rows, cols)
        diagonal = (k * devices + me >= first_diagonal).astype(jnp.int32).reshape(1)
        result = ladder(diagonal, blocks, factors, turned, core_matrix)
        returned.append(exchange(result.reshape(devices, 2, rows, cols)))
    residual = None
    for k in range(chunks):
        residual = place(
            returned[k].reshape(slots, rows, cols), residual, order[k * slots:(k + 1) * slots], pairs
        )
    return residual.reshape(amplitudes.shape)


def solution(mesh):
    return jax.shard_map(
        local,
        mesh=mesh,
        in_specs=(P(None, None, "row", "col"), P(), P(), P()),
        out_specs=P(None, None, "row", "col"),
        check_vma=False,
    )
```

```python
import functools

import jax
import jax.numpy as jnp
import numpy as np
from jax import lax
from jax.experimental import pallas as pl
from jax.experimental.pallas import tpu as pltpu
from jax.sharding import PartitionSpec as P

VMEM_LIMIT = 60 * 1024 * 1024


def couple_order(occupied):
    listing = []
    for first in range(occupied):
        for second in range(first + 1, occupied):
            listing += [first * occupied + second, second * occupied + first]
    listing += [first * occupied + first for first in range(occupied)]
    return np.array(listing, dtype=np.int32)


def hole_kernel(weights_ref, amplitudes_ref, out_ref):
    weights = weights_ref[...]
    slots = weights.shape[0]
    high = weights.astype(jnp.bfloat16)
    low = (weights - high.astype(jnp.float32)).astype(jnp.bfloat16)
    both = jnp.concatenate([high, low], axis=0)
    by_row = jnp.swapaxes(amplitudes_ref[...], 0, 1)
    terms = []
    for row in range(by_row.shape[0]):
        values = by_row[row]
        top = values.astype(jnp.bfloat16)
        rest = (values - top.astype(jnp.float32)).astype(jnp.bfloat16)
        main = jnp.dot(both, top, preferred_element_type=jnp.float32)
        small = jnp.dot(high, rest, preferred_element_type=jnp.float32)
        terms.append(main[:slots] + (main[slots:] + small))
    out_ref[...] = jnp.swapaxes(jnp.stack(terms, axis=0), 0, 1)


def hole(weights, amplitudes):
    slots, pairs = weights.shape
    _, rows, cols = amplitudes.shape
    step = 8
    return pl.pallas_call(
        hole_kernel,
        grid=(rows // step,),
        in_specs=[
            pl.BlockSpec((slots, pairs), lambda i: (0, 0)),
            pl.BlockSpec((pairs, step, cols), lambda i: (0, i, 0)),
        ],
        out_specs=pl.BlockSpec((slots, step, cols), lambda i: (0, i, 0)),
        out_shape=jax.ShapeDtypeStruct((slots, rows, cols), jnp.float32),
        compiler_params=pltpu.CompilerParams(vmem_limit_bytes=VMEM_LIMIT),
        cost_estimate=pl.CostEstimate(
            flops=6 * slots * pairs * rows * cols,
            bytes_accessed=4 * (slots + pairs) * rows * cols,
            transcendentals=0,
        ),
        name="hole",
    )(weights, amplitudes)


def ladder_kernel(diagonal_ref, blocks_ref, factors_ref, turned_ref, core_ref, out_ref,
                  summed, left, weighted):
    row_count, col_count, _, rows, cols = blocks_ref.shape
    virtual = row_count * rows
    grid_points = factors_ref.shape[1]
    tile = 256
    row_blocks = tile // rows
    col_blocks = tile // cols
    tiles = virtual // tile

    def one(which, _):
        partner = jnp.where(diagonal_ref[0] != 0, which, 1 - which)

        def first(t, _):
            span = pl.ds(pl.multiple_of(t * tile, tile), tile)
            for c in range(tiles):
                straight = jnp.concatenate(
                    [
                        jnp.concatenate(
                            [blocks_ref[t * row_blocks + r, c * col_blocks + q, which] for q in range(col_blocks)],
                            axis=1,
                        )
                        for r in range(row_blocks)
                    ],
                    axis=0,
                )
                other = jnp.concatenate(
                    [
                        jnp.concatenate(
                            [blocks_ref[c * row_blocks + r, t * col_blocks + q, partner] for q in range(col_blocks)],
                            axis=1,
                        )
                        for r in range(row_blocks)
                    ],
                    axis=0,
                )
                summed[span, c * tile:(c + 1) * tile] = straight + other.T
            left[span, :] = jnp.dot(
                summed[span, :].astype(jnp.bfloat16), factors_ref[...], preferred_element_type=jnp.float32
            ).astype(jnp.bfloat16)
            return 0

        lax.fori_loop(0, tiles, first, 0)

        def second(t, _):
            span = pl.ds(pl.multiple_of(t * tile, tile), tile)
            inner = jnp.dot(turned_ref[span, :], left[...], preferred_element_type=jnp.float32)
            weighted[span, :] = (core_ref[span, :] * inner).astype(jnp.bfloat16)
            return 0

        lax.fori_loop(0, grid_points // tile, second, 0)

        def third(t, _):
            span = pl.ds(pl.multiple_of(t * tile, tile), tile)
            spread = jnp.dot(
                factors_ref[span, :], weighted[...], preferred_element_type=jnp.float32
            ).astype(jnp.bfloat16)
            result = summed[span, :] + jnp.dot(spread, turned_ref[...], preferred_element_type=jnp.float32)
            for r in range(row_blocks):
                for c in range(col_count):
                    out_ref[t * row_blocks + r, c, which] = result[r * rows:(r + 1) * rows, c * cols:(c + 1) * cols]
            return 0

        lax.fori_loop(0, tiles, third, 0)
        return 0

    lax.fori_loop(0, 2, one, 0)


def ladder(diagonal, blocks, factors, turned, core_matrix):
    row_count, _, _, rows, _ = blocks.shape
    virtual = row_count * rows
    grid_points = factors.shape[1]
    vmem = pl.BlockSpec(memory_space=pltpu.VMEM)
    return pl.pallas_call(
        ladder_kernel,
        in_specs=[pl.BlockSpec(memory_space=pltpu.SMEM), vmem, vmem, vmem, vmem],
        out_specs=vmem,
        out_shape=jax.ShapeDtypeStruct(blocks.shape, jnp.float32),
        scratch_shapes=[
            pltpu.VMEM((virtual, virtual), jnp.float32),
            pltpu.VMEM((virtual, grid_points), jnp.bfloat16),
            pltpu.VMEM((grid_points, grid_points), jnp.bfloat16),
        ],
        compiler_params=pltpu.CompilerParams(vmem_limit_bytes=VMEM_LIMIT),
        cost_estimate=pl.CostEstimate(
            flops=16 * virtual * virtual * grid_points,
            bytes_accessed=24 * virtual * virtual,
            transcendentals=0,
        ),
        name="ladder",
    )(diagonal, blocks, factors, turned, core_matrix)


def place_kernel(places, group, blocks_ref, *refs):
    out_ref, held, in_sems, out_sems = refs[-4:]
    slots = len(places)

    def fetch(g):
        span = pl.ds(g * group, group)
        return pltpu.make_async_copy(blocks_ref.at[span], held.at[span], in_sems.at[g])

    def put(s):
        return pltpu.make_async_copy(held.at[s], out_ref.at[places[s]], out_sems.at[s])

    for g in range(slots // group):
        fetch(g).start()
    for g in range(slots // group):
        fetch(g).wait()
        for s in range(g * group, (g + 1) * group):
            put(s).start()
    for s in range(slots):
        put(s).wait()


def place(blocks, target, places, pairs):
    slots, rows, cols = blocks.shape
    group = max(1, slots // 8)
    hbm = pl.BlockSpec(memory_space=pl.ANY)
    operands = (blocks,) if target is None else (blocks, target)
    return pl.pallas_call(
        functools.partial(place_kernel, [int(p) for p in places], group),
        in_specs=[hbm] * len(operands),
        out_specs=hbm,
        out_shape=jax.ShapeDtypeStruct((pairs, rows, cols), jnp.float32),
        scratch_shapes=[
            pltpu.VMEM((slots, rows, cols), jnp.float32),
            pltpu.SemaphoreType.DMA((slots // group,)),
            pltpu.SemaphoreType.DMA((slots,)),
        ],
        input_output_aliases={} if target is None else {1: 0},
        compiler_params=pltpu.CompilerParams(vmem_limit_bytes=VMEM_LIMIT),
        cost_estimate=pl.CostEstimate(flops=0, bytes_accessed=8 * slots * rows * cols, transcendentals=0),
        name="place",
    )(*operands)


def exchange(blocks):
    return lax.all_to_all(blocks, ("row", "col"), split_axis=0, concat_axis=0, tiled=True)


MESH = pl.DeviceIdType.MESH


def pairs_of(step, column, slot, occupied):
    odd = occupied - 1
    first = lax.select(column == 0, jnp.int32(odd), lax.rem(step + column, odd))
    second = lax.select(column == 0, step, lax.rem(step + odd - column, odd))
    straight = lax.select(slot == 0, first * occupied + second, second * occupied + first)
    alone = (slot * (occupied // 2) + column) * (occupied + 1)
    return lax.select(step == odd, alone, straight)


def halves_kernel(weights_ref, amplitudes_ref, factors_hbm, core_hbm,
                  out_ref, slabs_ref, outer_ref, raw_ref, square_ref,
                  tiles, stage, chosen, factors, turned, core, core_turned, weighted, weighted_turned,
                  left, summed, held, other, right, right_turned, result, packing, squares,
                  tile_sems, stage_sem, slab_sems, open_sems, relay_send, relay_recv, raw_send, raw_recv,
                  square_send, square_recv, result_send, kept_sems, out_sems, load_sems):
    row = lax.axis_index("row")
    z = lax.axis_index("col")
    pairs, rows, cols = amplitudes_ref.shape
    steps, _, columns, _, _ = slabs_ref.shape
    occupied = steps
    virtual = columns * rows
    half = virtual // 2
    tile = half // 2
    per = tile // rows
    upper = z // 2
    inner = (z == 1) | (z == 2)
    mate = z + 1 - 2 * lax.rem(z, 2)
    across = 3 - z
    own_plane = 1 - upper
    own_rows = pl.multiple_of(upper * half, half)
    far_rows = pl.multiple_of(half - upper * half, half)
    rows_in_half = columns // 2
    own_first = upper * rows_in_half
    far_first = rows_in_half - own_first
    group = stage.shape[0] // (2 * columns)
    chunks = open_sems.shape[1]
    chunk_rows = rows // chunks
    blocks = rows // 8

    barrier = pltpu.get_barrier_semaphore()
    for d in range(1, columns):
        pl.semaphore_signal(barrier, 1, device_id=(lax.rem(row + d, columns), z), device_id_type=MESH)
    for d in range(columns):
        pl.semaphore_signal(barrier, 1, device_id=(d, mate), device_id_type=MESH)

    @pl.when(inner)
    def _():
        pl.semaphore_signal(barrier, 1, device_id=(row, across), device_id_type=MESH)

    def fetch(b, slot):
        return pltpu.make_async_copy(
            amplitudes_ref.at[:, pl.ds(pl.multiple_of(b * 8, 8), 8), :], tiles.at[slot], tile_sems.at[slot]
        )

    def sent_stage():
        part = stage.at[pl.ds(0, 2 * group * (columns - 1))]
        return pltpu.make_async_copy(part, part, stage_sem)

    def choose(g):
        fetch(0, 0).start()

        def take(n, _):
            step = g * group + n // (2 * columns)
            pair = pairs_of(step, lax.rem(n // 2, columns), lax.rem(n, 2), occupied)
            chosen[pl.ds(n, 1), :] = weights_ref[pl.ds(pair, 1), :]
            return 0

        lax.fori_loop(0, chosen.shape[0], take, 0)

    def hole_rows(start, count):
        weights = chosen[...]
        slots = weights.shape[0]
        high = weights.astype(jnp.bfloat16)
        low = (weights - high.astype(jnp.float32)).astype(jnp.bfloat16)
        both = jnp.concatenate([high, low], axis=0)

        def block(n, _):
            b = start + n
            slot = lax.rem(b, 2)

            @pl.when(b + 1 < blocks)
            def _():
                fetch(b + 1, 1 - slot).start()

            fetch(b, slot).wait()
            by_row = jnp.swapaxes(tiles[slot], 0, 1)
            terms = []
            for m in range(8):
                values = by_row[m]
                top = values.astype(jnp.bfloat16)
                rest = (values - top.astype(jnp.float32)).astype(jnp.bfloat16)
                main = jnp.dot(both, top, preferred_element_type=jnp.float32)
                small = jnp.dot(high, rest, preferred_element_type=jnp.float32)
                terms.append(main[:slots] + (main[slots:] + small))
            stage[:, pl.ds(pl.multiple_of(b * 8, 8), 8), :] = jnp.swapaxes(jnp.stack(terms, axis=0), 0, 1)
            return 0

        lax.fori_loop(0, count, block, 0)

    def send_tiles(n, step, span, arrival):
        for d in range(1, columns):
            to = lax.rem(row + d, columns)
            pltpu.make_async_remote_copy(
                src_ref=stage.at[pl.ds((n * columns + to) * 2, 2), span, :],
                dst_ref=slabs_ref.at[step, :, row, span, :],
                send_sem=stage_sem,
                recv_sem=arrival,
                device_id=(to, z),
                device_id_type=MESH,
            ).start()
        pltpu.make_async_copy(
            stage.at[pl.ds((n * columns + row) * 2, 2), span, :], slabs_ref.at[step, :, row, span, :], arrival
        ).start()

    def hole_group(g):
        choose(g)
        sent_stage().wait()
        hole_rows(0, blocks)

        def send(n, _):
            step = g * group + n
            send_tiles(n, step, pl.ds(0, rows), slab_sems.at[step])
            return 0

        lax.fori_loop(0, group, send, 0)

    def chunk_of(c):
        return pl.ds(pl.multiple_of(c * chunk_rows, chunk_rows), chunk_rows)

    def forward_chunk(step, c):
        span = chunk_of(c)
        part = slabs_ref.at[step, :, :, span, :]
        pltpu.make_async_copy(part, part, open_sems.at[step, c]).wait()

        @pl.when(inner)
        def _():
            pltpu.make_async_remote_copy(
                src_ref=slabs_ref.at[step, :, pl.ds(far_first, rows_in_half), span, :],
                dst_ref=raw_ref.at[step, own_plane, :, :, span, :],
                send_sem=raw_send.at[2 * step + own_plane], recv_sem=raw_recv.at[2 * step + own_plane],
                device_id=(row, across), device_id_type=MESH,
            ).start()

        @pl.when(jnp.logical_not(inner))
        def _():
            pltpu.make_async_remote_copy(
                src_ref=part, dst_ref=outer_ref.at[step, :, :, span, :],
                send_sem=relay_send.at[step], recv_sem=relay_recv.at[step],
                device_id=(row, mate), device_id_type=MESH,
            ).start()

    def opening():
        choose(0)
        hole_rows(0, blocks // chunks)

        @pl.when(inner)
        def _():
            pl.semaphore_wait(barrier, 2 * columns)

        @pl.when(jnp.logical_not(inner))
        def _():
            pl.semaphore_wait(barrier, 2 * columns - 1)

        def chunk(c, _):
            send_tiles(0, 0, chunk_of(c), open_sems.at[0, c])

            @pl.when(c >= 2)
            def _():
                forward_chunk(0, c - 2)

            @pl.when(c + 1 < chunks)
            def _():
                hole_rows((c + 1) * (blocks // chunks), blocks // chunks)

            return 0

        lax.fori_loop(0, chunks, chunk, 0)

        def follow(c, _):
            step = lax.select(c < 2, jnp.int32(0), jnp.int32(1))
            forward_chunk(step, lax.rem(c + chunks - 2, chunks))
            send_tiles(1, 1, chunk_of(c), open_sems.at[1, c])
            return 0

        lax.fori_loop(0, chunks, follow, 0)

        @pl.when(inner)
        def _():
            prepare()

        for c in range(chunks - 2, chunks):
            forward_chunk(1, c)

    def wait_slab(step):
        pltpu.make_async_copy(slabs_ref.at[step], slabs_ref.at[step], slab_sems.at[step]).wait()

    def relay(step):
        return pltpu.make_async_remote_copy(
            src_ref=slabs_ref.at[step], dst_ref=outer_ref.at[step],
            send_sem=relay_send.at[step], recv_sem=relay_recv.at[step],
            device_id=(row, mate), device_id_type=MESH,
        )

    def raw(source, step, plane):
        return pltpu.make_async_remote_copy(
            src_ref=source.at[step, :, pl.ds(far_first, rows_in_half)], dst_ref=raw_ref.at[step, plane],
            send_sem=raw_send.at[2 * step + plane], recv_sem=raw_recv.at[2 * step + plane],
            device_id=(row, across), device_id_type=MESH,
        )

    def square_copy(item, span, across_span):
        slot = lax.rem(item, 2)
        return pltpu.make_async_remote_copy(
            src_ref=squares.at[slot, span, across_span], dst_ref=square_ref.at[item, span, across_span],
            send_sem=square_send.at[slot], recv_sem=square_recv.at[item],
            device_id=(row, across), device_id_type=MESH,
        )

    strips = [(pl.ds(s * rows, rows), pl.ds(s * rows, half - s * rows)) for s in range(half // rows)]
    everything = pl.ds(0, half)
    strip_bytes_rows = sum((half - s * rows) * rows for s in range(half // rows)) // half

    def square(item):
        return square_copy(item, everything, everything)

    def strips_of(item):
        return square_copy(item, pl.ds(0, strip_bytes_rows), everything)

    def item_of(item):
        alone = item >= steps - 1
        step = jnp.minimum(item, steps - 1)
        straight = lax.select(alone, item - (steps - 1), jnp.int32(0))
        flipped = lax.select(alone, item - (steps - 1), jnp.int32(1))
        return alone, step, straight, flipped

    def raw_own(step):
        wait_slab(step)
        raw(slabs_ref, step, own_plane).start()

    def pack(item):
        alone, step, straight, flipped = item_of(item)

        @pl.when(item < steps)
        def _():
            relay(step).wait_recv()
            raw(outer_ref, step, 1 - own_plane).start()

        mine = pltpu.make_async_copy(
            slabs_ref.at[step, :, pl.ds(own_first, rows_in_half)], packing.at[own_plane], load_sems.at[0])
        theirs = pltpu.make_async_copy(
            outer_ref.at[step, :, pl.ds(own_first, rows_in_half)], packing.at[1 - own_plane], load_sems.at[1])
        mine.start()
        theirs.start()

        @pl.when(item >= 2)
        def _():
            square(item).wait_send()

        mine.wait()
        theirs.wait()
        slot = lax.rem(item, 2)
        for a in range(2):
            for b in range(2):
                squares[slot, a * tile:(a + 1) * tile, b * tile:(b + 1) * tile] = (
                    packing[b, straight, a * per:(a + 1) * per].reshape(tile, cols)
                    + packing[a, flipped, b * per:(b + 1) * per].reshape(tile, cols).T
                )

        @pl.when(jnp.logical_not(alone))
        def _():
            square(item).start()

        @pl.when(alone)
        def _():
            for span, across_span in strips:
                square_copy(item, span, across_span).start()

    def prepare():
        top = pltpu.make_async_copy(
            factors_hbm.at[pl.ds(own_rows, half), :], factors.at[pl.ds(0, half), :], load_sems.at[0])
        bottom = pltpu.make_async_copy(
            factors_hbm.at[pl.ds(far_rows, half), :], factors.at[pl.ds(half, half), :], load_sems.at[1])
        whole = pltpu.make_async_copy(core_hbm, core, load_sems.at[2])
        for copy in (top, bottom, whole):
            copy.start()
        for copy in (top, bottom, whole):
            copy.wait()

        def turn(t, _):
            span = pl.ds(pl.multiple_of(t * tile, tile), tile)
            for c in range(virtual // tile):
                turned[c * tile:(c + 1) * tile, span] = factors[span, c * tile:(c + 1) * tile].T
                core_turned[c * tile:(c + 1) * tile, span] = core[span, c * tile:(c + 1) * tile].T
            return 0

        lax.fori_loop(0, virtual // tile, turn, 0)

    def kept_result(slot, pair):
        return pltpu.make_async_copy(
            result.at[slot, own_plane * columns + lax.rem(row + own_first, columns)],
            out_ref.at[pair], kept_sems.at[slot])

    def sent_result(slot):
        part = result.at[slot, pl.ds(0, 2 * columns - 1)]
        pltpu.make_async_copy(part, part, result_send.at[slot]).wait()
        kept_result(slot, 0).wait()

    def give(item_step, slot, t):
        pair = pairs_of(item_step, row, slot, occupied)
        for n in range(per):
            q = t * per + n
            to = lax.rem(q + own_first, columns)
            for p in range(2):
                plane = lax.rem(own_plane + 1 + p, 2)
                where = lax.select(own_plane == plane, z, mate)

                @pl.when((own_plane != plane) | (to != row))
                def _():
                    pltpu.make_async_remote_copy(
                        src_ref=result.at[slot, plane * columns + q], dst_ref=out_ref.at[pair],
                        send_sem=result_send.at[slot], recv_sem=out_sems.at[item_step],
                        device_id=(to, where), device_id_type=MESH,
                    ).start()

    def keep(item_step, slot):
        kept_result(slot, pairs_of(item_step, row, slot, occupied)).start()

    def ladder_item(item):
        alone, step, straight, flipped = item_of(item)
        loads = [
            pltpu.make_async_copy(
                slabs_ref.at[step, :, pl.ds(own_first, rows_in_half)], held.at[own_plane, :, pl.ds(0, rows_in_half)],
                load_sems.at[0]),
            pltpu.make_async_copy(
                slabs_ref.at[step, :, pl.ds(far_first, rows_in_half)],
                held.at[own_plane, :, pl.ds(rows_in_half, rows_in_half)], load_sems.at[1]),
            pltpu.make_async_copy(
                outer_ref.at[step, :, pl.ds(own_first, rows_in_half)],
                held.at[1 - own_plane, :, pl.ds(0, rows_in_half)], load_sems.at[2]),
            pltpu.make_async_copy(
                outer_ref.at[step, :, pl.ds(far_first, rows_in_half)],
                held.at[1 - own_plane, :, pl.ds(rows_in_half, rows_in_half)], load_sems.at[3]),
        ]
        for copy in loads:
            copy.start()

        @pl.when(item < steps)
        def _():
            raw(slabs_ref, step, 0).wait_recv()
            raw(slabs_ref, step, 1).wait_recv()

        received = pltpu.make_async_copy(raw_ref.at[step], other, load_sems.at[4])
        received.start()
        for copy in loads + [received]:
            copy.wait()

        def square_load(span, across_span, sem):
            return pltpu.make_async_copy(
                square_ref.at[item, span, across_span],
                summed.at[pl.ds(half + span.start, span.size), pl.ds(half + across_span.start, across_span.size)],
                load_sems.at[sem])

        def assemble():
            for a in range(2):
                for b in range(2):
                    here = slice(a * tile, (a + 1) * tile)
                    there = slice(half + b * tile, half + (b + 1) * tile)
                    here_rows = slice(a * per, (a + 1) * per)
                    near_rows = slice(b * per, (b + 1) * per)
                    there_rows = slice(rows_in_half + b * per, rows_in_half + (b + 1) * per)

                    def block(ref, plane, slot, which):
                        return ref[plane, slot, which].reshape(tile, cols)

                    summed[here, b * tile:(b + 1) * tile] = (
                        block(held, b, straight, here_rows) + block(held, a, flipped, near_rows).T)
                    summed[here, there] = block(other, b, straight, here_rows) + block(held, a, flipped, there_rows).T
                    summed[there, here] = block(held, a, straight, there_rows) + block(other, b, flipped, here_rows).T

        assemble()

        @pl.when(jnp.logical_not(alone))
        def _():
            square(item).wait_recv()
            load = square_load(everything, everything, 5)
            load.start()
            load.wait()

        @pl.when(alone)
        def _():
            strips_of(item).wait_recv()
            copies = [square_load(span, across_span, 5 + n) for n, (span, across_span) in enumerate(strips)]
            for copy in copies:
                copy.start()
            for copy in copies:
                copy.wait()
            for a in range(1, half // rows):
                for b in range(a):
                    down = slice(half + a * rows, half + (a + 1) * rows)
                    along = slice(half + b * rows, half + (b + 1) * rows)
                    summed[down, along] = summed[along, down].T

        def first(t, _):
            span = pl.ds(pl.multiple_of(t * tile, tile), tile)
            left[span, :] = jnp.dot(
                summed[span, :].astype(jnp.bfloat16), factors[...], preferred_element_type=jnp.float32
            ).astype(jnp.bfloat16)
            return 0

        lax.fori_loop(0, virtual // tile, first, 0)

        def second(t, _):
            span = pl.ds(pl.multiple_of(t * tile, tile), tile)
            product = jnp.dot(turned[span, :], left[...], preferred_element_type=jnp.float32)
            weighted[span, :] = (core[span, :] * product).astype(jnp.bfloat16)
            weighted_turned[span, :] = (core_turned[span, :] * product).astype(jnp.bfloat16)
            return 0

        lax.fori_loop(0, virtual // tile, second, 0)

        def third(t, _):
            span = pl.ds(pl.multiple_of(t * tile, tile), tile)
            right[span, :] = jnp.dot(
                weighted[span, :], turned[:, 0:half], preferred_element_type=jnp.float32
            ).astype(jnp.bfloat16)
            return 0

        lax.fori_loop(0, virtual // tile, third, 0)

        @pl.when((item > 0) & (item <= steps - 1))
        def _():
            sent_result(0)

        @pl.when(((item > 0) & (item < steps - 1)) | (item == steps))
        def _():
            sent_result(1)

        def fourth(t, _):
            span = pl.ds(pl.multiple_of(t * tile, tile), tile)
            value = summed[span, 0:half] + jnp.dot(
                factors[span, :], right[...], preferred_element_type=jnp.float32)
            for p in range(2):
                for n in range(per):
                    result[straight, p * columns + t * per + n] = (
                        value[n * rows:(n + 1) * rows, p * tile:(p + 1) * tile])
            give(step, straight, t)
            return 0

        lax.fori_loop(0, virtual // tile, fourth, 0)
        keep(step, straight)

        @pl.when(jnp.logical_not(alone))
        def _():
            for b in range(2):
                right_turned[b * tile:(b + 1) * tile, :] = jnp.dot(
                    factors[b * tile:(b + 1) * tile, :], weighted_turned[...], preferred_element_type=jnp.float32
                ).astype(jnp.bfloat16)

            def fifth(t, _):
                span = pl.ds(pl.multiple_of(t * tile, tile), tile)
                for p in range(2):
                    value = summed[p * tile:(p + 1) * tile, span] + jnp.dot(
                        right_turned[p * tile:(p + 1) * tile, :], turned[:, span],
                        preferred_element_type=jnp.float32)
                    value = value.T
                    for n in range(per):
                        result[1, p * columns + t * per + n] = value[n * rows:(n + 1) * rows, :]
                give(step, 1, t)
                return 0

            lax.fori_loop(0, virtual // tile, fifth, 0)
            keep(step, 1)

    groups = steps // group
    opening()

    @pl.when(jnp.logical_not(inner))
    def _():
        def outer_group(g, _):
            hole_group(g)
            for n in range(group):
                wait_slab(g * group + n)
                relay(g * group + n).start()
            return 0

        lax.fori_loop(1, groups, outer_group, 0)

        def finish(step, _):
            relay(step).wait_send()
            return 0

        lax.fori_loop(0, steps, finish, 0)

    @pl.when(inner)
    def _():
        pack(0)

        def body(item, _):
            @pl.when((lax.rem(item, group) == 0) & (item < steps - group))
            def _():
                hole_group(item // group + 1)

            @pl.when(item < steps)
            def _():
                pack(item + 1)

            ladder_item(item)

            @pl.when(item + 2 < steps)
            def _():
                raw_own(item + 2)

            return 0

        lax.fori_loop(0, steps + 1, body, 0)

        def finish(n, _):
            raw(slabs_ref, n // 2, lax.rem(n, 2)).wait_send()
            return 0

        lax.fori_loop(0, 2 * steps, finish, 0)
        strips_of(steps - 1).wait_send()
        strips_of(steps).wait_send()
        sent_result(0)
        sent_result(1)

    sent_stage().wait()

    def arrived(tiles_of_step):
        def wait(step, _):
            part = out_ref.at[pl.ds(0, tiles_of_step)]
            pltpu.make_async_copy(part, part, out_sems.at[step]).wait()
            return 0

        lax.fori_loop(0, steps, wait, 0)

    @pl.when(inner)
    def _():
        arrived(2 * (columns - 1))

    @pl.when(jnp.logical_not(inner))
    def _():
        arrived(2 * columns)


def halves(amplitudes, hole_ints, factors, core_matrix, columns):
    occupied, _, rows, cols = amplitudes.shape
    pairs = occupied * occupied
    virtual = factors.shape[0]
    grid_points = factors.shape[1]
    steps = occupied
    half = virtual // 2
    tile = half // 2
    group = 2
    f32, bf16 = jnp.float32, jnp.bfloat16
    hbm = pl.BlockSpec(memory_space=pl.ANY)
    vmem = pl.BlockSpec(memory_space=pltpu.VMEM)
    dma = pltpu.SemaphoreType.DMA
    outs = pl.pallas_call(
        halves_kernel,
        in_specs=[vmem, hbm, hbm, hbm],
        out_specs=[hbm] * 5,
        out_shape=[
            jax.ShapeDtypeStruct((pairs, rows, cols), f32),
            jax.ShapeDtypeStruct((steps, 2, columns, rows, cols), f32),
            jax.ShapeDtypeStruct((steps, 2, columns, rows, cols), f32),
            jax.ShapeDtypeStruct((steps, 2, 2, columns // 2, rows, cols), f32),
            jax.ShapeDtypeStruct((steps + 1, half, half), f32),
        ],
        scratch_shapes=[
            pltpu.VMEM((2, pairs, 8, cols), f32),
            pltpu.VMEM((group * 2 * columns, rows, cols), f32),
            pltpu.VMEM((group * 2 * columns, pairs), f32),
            pltpu.VMEM((virtual, grid_points), bf16),
            pltpu.VMEM((grid_points, virtual), bf16),
            pltpu.VMEM((grid_points, grid_points), f32),
            pltpu.VMEM((grid_points, grid_points), f32),
            pltpu.VMEM((grid_points, grid_points), bf16),
            pltpu.VMEM((grid_points, grid_points), bf16),
            pltpu.VMEM((virtual, grid_points), bf16),
            pltpu.VMEM((virtual, virtual), f32),
            pltpu.VMEM((2, 2, columns, rows, cols), f32),
            pltpu.VMEM((2, 2, columns // 2, rows, cols), f32),
            pltpu.VMEM((grid_points, half), bf16),
            pltpu.VMEM((half, grid_points), bf16),
            pltpu.VMEM((2, 2 * columns, rows, cols), f32),
            pltpu.VMEM((2, 2, columns // 2, rows, cols), f32),
            pltpu.VMEM((2, half, half), f32),
            dma((2,)),
            dma,
            dma((steps,)),
            dma((group, 4)),
            dma((steps,)),
            dma((steps,)),
            dma((2 * steps,)),
            dma((2 * steps,)),
            dma((2,)),
            dma((steps + 1,)),
            dma((2,)),
            dma((2,)),
            dma((steps,)),
            dma((5 + half // rows,)),
        ],
        compiler_params=pltpu.CompilerParams(
            vmem_limit_bytes=VMEM_LIMIT, collective_id=0, has_side_effects=True),
        name="halves",
    )(hole_ints, amplitudes.reshape(pairs, rows, cols), factors, core_matrix)
    return outs[0].reshape(amplitudes.shape)


def local(amplitudes, hole_ints, factors, core_matrix):
    row_count = lax.axis_size("row")
    col_count = lax.axis_size("col")
    devices = row_count * col_count
    occupied, _, rows, cols = amplitudes.shape
    if (row_count, col_count, occupied, rows, cols) == (8, 4, 16, 128, 256):
        return halves(amplitudes, hole_ints, factors, core_matrix, row_count)
    pairs = occupied * occupied
    chunks = pairs // (2 * devices)
    slots = 2 * devices
    flattened = amplitudes.reshape(pairs, rows, cols)
    order = couple_order(occupied)
    weights = jnp.take(hole_ints, jnp.asarray(order), axis=0)
    turned = factors.T
    me = lax.axis_index(("row", "col"))
    first_diagonal = occupied * (occupied - 1) // 2

    arrived = []
    for k in range(chunks):
        term = hole(weights[k * slots:(k + 1) * slots], flattened)
        arrived.append(exchange(term.reshape(devices, 2, rows, cols)))
    returned = []
    for k in range(chunks):
        blocks = arrived[k].reshape(row_count, col_count, 2, rows, cols)
        diagonal = (k * devices + me >= first_diagonal).astype(jnp.int32).reshape(1)
        result = ladder(diagonal, blocks, factors, turned, core_matrix)
        returned.append(exchange(result.reshape(devices, 2, rows, cols)))
    residual = None
    for k in range(chunks):
        residual = place(
            returned[k].reshape(slots, rows, cols), residual, order[k * slots:(k + 1) * slots], pairs
        )
    return residual.reshape(amplitudes.shape)


def solution(mesh):
    return jax.shard_map(
        local,
        mesh=mesh,
        in_specs=(P(None, None, "row", "col"), P(), P(), P()),
        out_specs=P(None, None, "row", "col"),
        check_vma=False,
    )
```

```python
import functools

import jax
import jax.numpy as jnp
import numpy as np
from jax import lax
from jax.experimental import pallas as pl
from jax.experimental.pallas import tpu as pltpu
from jax.sharding import PartitionSpec as P

VMEM_LIMIT = 60 * 1024 * 1024


def couple_order(occupied):
    listing = []
    for first in range(occupied):
        for second in range(first + 1, occupied):
            listing += [first * occupied + second, second * occupied + first]
    listing += [first * occupied + first for first in range(occupied)]
    return np.array(listing, dtype=np.int32)


def hole_kernel(weights_ref, amplitudes_ref, out_ref):
    weights = weights_ref[...]
    slots = weights.shape[0]
    high = weights.astype(jnp.bfloat16)
    low = (weights - high.astype(jnp.float32)).astype(jnp.bfloat16)
    both = jnp.concatenate([high, low], axis=0)
    by_row = jnp.swapaxes(amplitudes_ref[...], 0, 1)
    terms = []
    for row in range(by_row.shape[0]):
        values = by_row[row]
        top = values.astype(jnp.bfloat16)
        rest = (values - top.astype(jnp.float32)).astype(jnp.bfloat16)
        main = jnp.dot(both, top, preferred_element_type=jnp.float32)
        small = jnp.dot(high, rest, preferred_element_type=jnp.float32)
        terms.append(main[:slots] + (main[slots:] + small))
    out_ref[...] = jnp.swapaxes(jnp.stack(terms, axis=0), 0, 1)


def hole(weights, amplitudes):
    slots, pairs = weights.shape
    _, rows, cols = amplitudes.shape
    step = 8
    return pl.pallas_call(
        hole_kernel,
        grid=(rows // step,),
        in_specs=[
            pl.BlockSpec((slots, pairs), lambda i: (0, 0)),
            pl.BlockSpec((pairs, step, cols), lambda i: (0, i, 0)),
        ],
        out_specs=pl.BlockSpec((slots, step, cols), lambda i: (0, i, 0)),
        out_shape=jax.ShapeDtypeStruct((slots, rows, cols), jnp.float32),
        compiler_params=pltpu.CompilerParams(vmem_limit_bytes=VMEM_LIMIT),
        cost_estimate=pl.CostEstimate(
            flops=6 * slots * pairs * rows * cols,
            bytes_accessed=4 * (slots + pairs) * rows * cols,
            transcendentals=0,
        ),
        name="hole",
    )(weights, amplitudes)


def ladder_kernel(diagonal_ref, blocks_ref, factors_ref, turned_ref, core_ref, out_ref,
                  summed, left, weighted):
    row_count, col_count, _, rows, cols = blocks_ref.shape
    virtual = row_count * rows
    grid_points = factors_ref.shape[1]
    tile = 256
    row_blocks = tile // rows
    col_blocks = tile // cols
    tiles = virtual // tile

    def one(which, _):
        partner = jnp.where(diagonal_ref[0] != 0, which, 1 - which)

        def first(t, _):
            span = pl.ds(pl.multiple_of(t * tile, tile), tile)
            for c in range(tiles):
                straight = jnp.concatenate(
                    [
                        jnp.concatenate(
                            [blocks_ref[t * row_blocks + r, c * col_blocks + q, which] for q in range(col_blocks)],
                            axis=1,
                        )
                        for r in range(row_blocks)
                    ],
                    axis=0,
                )
                other = jnp.concatenate(
                    [
                        jnp.concatenate(
                            [blocks_ref[c * row_blocks + r, t * col_blocks + q, partner] for q in range(col_blocks)],
                            axis=1,
                        )
                        for r in range(row_blocks)
                    ],
                    axis=0,
                )
                summed[span, c * tile:(c + 1) * tile] = straight + other.T
            left[span, :] = jnp.dot(
                summed[span, :].astype(jnp.bfloat16), factors_ref[...], preferred_element_type=jnp.float32
            ).astype(jnp.bfloat16)
            return 0

        lax.fori_loop(0, tiles, first, 0)

        def second(t, _):
            span = pl.ds(pl.multiple_of(t * tile, tile), tile)
            inner = jnp.dot(turned_ref[span, :], left[...], preferred_element_type=jnp.float32)
            weighted[span, :] = (core_ref[span, :] * inner).astype(jnp.bfloat16)
            return 0

        lax.fori_loop(0, grid_points // tile, second, 0)

        def third(t, _):
            span = pl.ds(pl.multiple_of(t * tile, tile), tile)
            spread = jnp.dot(
                factors_ref[span, :], weighted[...], preferred_element_type=jnp.float32
            ).astype(jnp.bfloat16)
            result = summed[span, :] + jnp.dot(spread, turned_ref[...], preferred_element_type=jnp.float32)
            for r in range(row_blocks):
                for c in range(col_count):
                    out_ref[t * row_blocks + r, c, which] = result[r * rows:(r + 1) * rows, c * cols:(c + 1) * cols]
            return 0

        lax.fori_loop(0, tiles, third, 0)
        return 0

    lax.fori_loop(0, 2, one, 0)


def ladder(diagonal, blocks, factors, turned, core_matrix):
    row_count, _, _, rows, _ = blocks.shape
    virtual = row_count * rows
    grid_points = factors.shape[1]
    vmem = pl.BlockSpec(memory_space=pltpu.VMEM)
    return pl.pallas_call(
        ladder_kernel,
        in_specs=[pl.BlockSpec(memory_space=pltpu.SMEM), vmem, vmem, vmem, vmem],
        out_specs=vmem,
        out_shape=jax.ShapeDtypeStruct(blocks.shape, jnp.float32),
        scratch_shapes=[
            pltpu.VMEM((virtual, virtual), jnp.float32),
            pltpu.VMEM((virtual, grid_points), jnp.bfloat16),
            pltpu.VMEM((grid_points, grid_points), jnp.bfloat16),
        ],
        compiler_params=pltpu.CompilerParams(vmem_limit_bytes=VMEM_LIMIT),
        cost_estimate=pl.CostEstimate(
            flops=16 * virtual * virtual * grid_points,
            bytes_accessed=24 * virtual * virtual,
            transcendentals=0,
        ),
        name="ladder",
    )(diagonal, blocks, factors, turned, core_matrix)


def place_kernel(places, group, blocks_ref, *refs):
    out_ref, held, in_sems, out_sems = refs[-4:]
    slots = len(places)

    def fetch(g):
        span = pl.ds(g * group, group)
        return pltpu.make_async_copy(blocks_ref.at[span], held.at[span], in_sems.at[g])

    def put(s):
        return pltpu.make_async_copy(held.at[s], out_ref.at[places[s]], out_sems.at[s])

    for g in range(slots // group):
        fetch(g).start()
    for g in range(slots // group):
        fetch(g).wait()
        for s in range(g * group, (g + 1) * group):
            put(s).start()
    for s in range(slots):
        put(s).wait()


def place(blocks, target, places, pairs):
    slots, rows, cols = blocks.shape
    group = max(1, slots // 8)
    hbm = pl.BlockSpec(memory_space=pl.ANY)
    operands = (blocks,) if target is None else (blocks, target)
    return pl.pallas_call(
        functools.partial(place_kernel, [int(p) for p in places], group),
        in_specs=[hbm] * len(operands),
        out_specs=hbm,
        out_shape=jax.ShapeDtypeStruct((pairs, rows, cols), jnp.float32),
        scratch_shapes=[
            pltpu.VMEM((slots, rows, cols), jnp.float32),
            pltpu.SemaphoreType.DMA((slots // group,)),
            pltpu.SemaphoreType.DMA((slots,)),
        ],
        input_output_aliases={} if target is None else {1: 0},
        compiler_params=pltpu.CompilerParams(vmem_limit_bytes=VMEM_LIMIT),
        cost_estimate=pl.CostEstimate(flops=0, bytes_accessed=8 * slots * rows * cols, transcendentals=0),
        name="place",
    )(*operands)


def exchange(blocks):
    return lax.all_to_all(blocks, ("row", "col"), split_axis=0, concat_axis=0, tiled=True)


MESH = pl.DeviceIdType.MESH


def pairs_of(step, column, slot, occupied):
    odd = occupied - 1
    first = lax.select(column == 0, jnp.int32(odd), lax.rem(step + column, odd))
    second = lax.select(column == 0, step, lax.rem(step + odd - column, odd))
    straight = lax.select(slot == 0, first * occupied + second, second * occupied + first)
    alone = (slot * (occupied // 2) + column) * (occupied + 1)
    return lax.select(step == odd, alone, straight)


def halves_kernel(weights_ref, amplitudes_ref, factors_hbm, core_hbm,
                  out_ref, slabs_ref, outer_ref, raw_ref, square_ref,
                  tiles, stage, chosen, factors, turned, core, core_turned, weighted, weighted_turned,
                  left, summed, held, other, right, right_turned, result, packing, squares,
                  tile_sems, stage_sem, slab_sems, open_sems, relay_send, relay_recv, raw_send, raw_recv,
                  square_send, square_recv, result_send, kept_sems, out_sems, load_sems):
    row = lax.axis_index("row")
    z = lax.axis_index("col")
    pairs, rows, cols = amplitudes_ref.shape
    steps, _, columns, _, _ = slabs_ref.shape
    occupied = steps
    virtual = columns * rows
    half = virtual // 2
    tile = half // 2
    per = tile // rows
    upper = z // 2
    inner = (z == 1) | (z == 2)
    mate = z + 1 - 2 * lax.rem(z, 2)
    across = 3 - z
    own_plane = 1 - upper
    own_rows = pl.multiple_of(upper * half, half)
    far_rows = pl.multiple_of(half - upper * half, half)
    rows_in_half = columns // 2
    own_first = upper * rows_in_half
    far_first = rows_in_half - own_first
    group = stage.shape[0] // (2 * columns)
    chunks = open_sems.shape[1]
    chunk_rows = rows // chunks
    blocks = rows // 8

    barrier = pltpu.get_barrier_semaphore()
    for d in range(1, columns):
        pl.semaphore_signal(barrier, 1, device_id=(lax.rem(row + d, columns), z), device_id_type=MESH)
    for d in range(columns):
        pl.semaphore_signal(barrier, 1, device_id=(d, mate), device_id_type=MESH)

    @pl.when(inner)
    def _():
        pl.semaphore_signal(barrier, 1, device_id=(row, across), device_id_type=MESH)

    def fetch(b, slot):
        return pltpu.make_async_copy(
            amplitudes_ref.at[:, pl.ds(pl.multiple_of(b * 8, 8), 8), :], tiles.at[slot], tile_sems.at[slot]
        )

    def sent_stage():
        part = stage.at[pl.ds(0, 2 * group * (columns - 1))]
        return pltpu.make_async_copy(part, part, stage_sem)

    def choose(g):
        fetch(0, 0).start()

        def take(n, _):
            step = g * group + n // (2 * columns)
            pair = pairs_of(step, lax.rem(n // 2, columns), lax.rem(n, 2), occupied)
            chosen[pl.ds(n, 1), :] = weights_ref[pl.ds(pair, 1), :]
            return 0

        lax.fori_loop(0, chosen.shape[0], take, 0)

    def hole_rows(start, count):
        weights = chosen[...]
        slots = weights.shape[0]
        high = weights.astype(jnp.bfloat16)
        low = (weights - high.astype(jnp.float32)).astype(jnp.bfloat16)
        both = jnp.concatenate([high, low], axis=0)

        def block(n, _):
            b = start + n
            slot = lax.rem(b, 2)

            @pl.when(b + 1 < blocks)
            def _():
                fetch(b + 1, 1 - slot).start()

            fetch(b, slot).wait()
            by_row = jnp.swapaxes(tiles[slot], 0, 1)
            terms = []
            for m in range(8):
                values = by_row[m]
                top = values.astype(jnp.bfloat16)
                rest = (values - top.astype(jnp.float32)).astype(jnp.bfloat16)
                main = jnp.dot(both, top, preferred_element_type=jnp.float32)
                small = jnp.dot(high, rest, preferred_element_type=jnp.float32)
                terms.append(main[:slots] + (main[slots:] + small))
            stage[:, pl.ds(pl.multiple_of(b * 8, 8), 8), :] = jnp.swapaxes(jnp.stack(terms, axis=0), 0, 1)
            return 0

        lax.fori_loop(0, count, block, 0)

    def send_tiles(n, step, span, arrival):
        for d in range(1, columns):
            to = lax.rem(row + d, columns)
            pltpu.make_async_remote_copy(
                src_ref=stage.at[pl.ds((n * columns + to) * 2, 2), span, :],
                dst_ref=slabs_ref.at[step, :, row, span, :],
                send_sem=stage_sem,
                recv_sem=arrival,
                device_id=(to, z),
                device_id_type=MESH,
            ).start()
        pltpu.make_async_copy(
            stage.at[pl.ds((n * columns + row) * 2, 2), span, :], slabs_ref.at[step, :, row, span, :], arrival
        ).start()

    def hole_group(g):
        choose(g)
        sent_stage().wait()
        hole_rows(0, blocks)

        def send(n, _):
            step = g * group + n
            send_tiles(n, step, pl.ds(0, rows), slab_sems.at[step])
            return 0

        lax.fori_loop(0, group, send, 0)

    def chunk_of(c):
        return pl.ds(pl.multiple_of(c * chunk_rows, chunk_rows), chunk_rows)

    def forward_chunk(step, c):
        span = chunk_of(c)
        part = slabs_ref.at[step, :, :, span, :]
        pltpu.make_async_copy(part, part, open_sems.at[step, c]).wait()

        @pl.when(inner)
        def _():
            pltpu.make_async_remote_copy(
                src_ref=slabs_ref.at[step, :, pl.ds(far_first, rows_in_half), span, :],
                dst_ref=raw_ref.at[step, own_plane, :, :, span, :],
                send_sem=raw_send.at[2 * step + own_plane], recv_sem=raw_recv.at[2 * step + own_plane],
                device_id=(row, across), device_id_type=MESH,
            ).start()

        @pl.when(jnp.logical_not(inner) & (step == 0))
        def _():
            pltpu.make_async_remote_copy(
                src_ref=part, dst_ref=outer_ref.at[step, :, :, span, :],
                send_sem=relay_send.at[step], recv_sem=relay_recv.at[step],
                device_id=(row, mate), device_id_type=MESH,
            ).start()

    def opening():
        window = 3
        choose(0)
        hole_rows(0, blocks // chunks)

        @pl.when(inner)
        def _():
            pl.semaphore_wait(barrier, 2 * columns)

        @pl.when(jnp.logical_not(inner))
        def _():
            pl.semaphore_wait(barrier, 2 * columns - 1)

        def chunk(c, _):
            send_tiles(0, 0, chunk_of(c), open_sems.at[0, c])

            @pl.when(c >= window)
            def _():
                forward_chunk(0, c - window)

            @pl.when(c + 1 < chunks)
            def _():
                hole_rows((c + 1) * (blocks // chunks), blocks // chunks)

            return 0

        lax.fori_loop(0, chunks, chunk, 0)

        def follow(c, _):
            step = lax.select(c < window, jnp.int32(0), jnp.int32(1))
            forward_chunk(step, lax.rem(c + chunks - window, chunks))
            send_tiles(1, 1, chunk_of(c), open_sems.at[1, c])
            return 0

        lax.fori_loop(0, chunks, follow, 0)

        @pl.when(inner)
        def _():
            prepare()

        for c in range(chunks - window, chunks):
            forward_chunk(1, c)

    def wait_slab(step):
        pltpu.make_async_copy(slabs_ref.at[step], slabs_ref.at[step], slab_sems.at[step]).wait()

    def relay(step):
        return pltpu.make_async_remote_copy(
            src_ref=slabs_ref.at[step], dst_ref=outer_ref.at[step],
            send_sem=relay_send.at[step], recv_sem=relay_recv.at[step],
            device_id=(row, mate), device_id_type=MESH,
        )

    def raw(source, step, plane):
        return pltpu.make_async_remote_copy(
            src_ref=source.at[step, :, pl.ds(far_first, rows_in_half)], dst_ref=raw_ref.at[step, plane],
            send_sem=raw_send.at[2 * step + plane], recv_sem=raw_recv.at[2 * step + plane],
            device_id=(row, across), device_id_type=MESH,
        )

    def square_copy(item, span, across_span):
        slot = lax.rem(item, 2)
        return pltpu.make_async_remote_copy(
            src_ref=squares.at[slot, span, across_span], dst_ref=square_ref.at[item, span, across_span],
            send_sem=square_send.at[slot], recv_sem=square_recv.at[item],
            device_id=(row, across), device_id_type=MESH,
        )

    strips = [(pl.ds(s * rows, rows), pl.ds(s * rows, half - s * rows)) for s in range(half // rows)]
    everything = pl.ds(0, half)
    strip_bytes_rows = sum((half - s * rows) * rows for s in range(half // rows)) // half

    def square(item):
        return square_copy(item, everything, everything)

    def strips_of(item):
        return square_copy(item, pl.ds(0, strip_bytes_rows), everything)

    def item_of(item):
        alone = item >= steps - 1
        step = jnp.minimum(item, steps - 1)
        straight = lax.select(alone, item - (steps - 1), jnp.int32(0))
        flipped = lax.select(alone, item - (steps - 1), jnp.int32(1))
        return alone, step, straight, flipped

    def raw_own(step):
        wait_slab(step)
        raw(slabs_ref, step, own_plane).start()

    def pack(item):
        alone, step, straight, flipped = item_of(item)

        @pl.when(item < steps)
        def _():
            relay(step).wait_recv()
            raw(outer_ref, step, 1 - own_plane).start()

        mine = pltpu.make_async_copy(
            slabs_ref.at[step, :, pl.ds(own_first, rows_in_half)], packing.at[own_plane], load_sems.at[0])
        theirs = pltpu.make_async_copy(
            outer_ref.at[step, :, pl.ds(own_first, rows_in_half)], packing.at[1 - own_plane], load_sems.at[1])
        mine.start()
        theirs.start()

        @pl.when(item >= 2)
        def _():
            square(item).wait_send()

        mine.wait()
        theirs.wait()
        slot = lax.rem(item, 2)
        for a in range(2):
            for b in range(2):
                squares[slot, a * tile:(a + 1) * tile, b * tile:(b + 1) * tile] = (
                    packing[b, straight, a * per:(a + 1) * per].reshape(tile, cols)
                    + packing[a, flipped, b * per:(b + 1) * per].reshape(tile, cols).T
                )

        @pl.when(jnp.logical_not(alone))
        def _():
            square(item).start()

        @pl.when(alone)
        def _():
            for span, across_span in strips:
                square_copy(item, span, across_span).start()

    def prepare():
        top = pltpu.make_async_copy(
            factors_hbm.at[pl.ds(own_rows, half), :], factors.at[pl.ds(0, half), :], load_sems.at[0])
        bottom = pltpu.make_async_copy(
            factors_hbm.at[pl.ds(far_rows, half), :], factors.at[pl.ds(half, half), :], load_sems.at[1])
        whole = pltpu.make_async_copy(core_hbm, core, load_sems.at[2])
        for copy in (top, bottom, whole):
            copy.start()
        for copy in (top, bottom, whole):
            copy.wait()

        def turn(t, _):
            span = pl.ds(pl.multiple_of(t * tile, tile), tile)
            for c in range(virtual // tile):
                turned[c * tile:(c + 1) * tile, span] = factors[span, c * tile:(c + 1) * tile].T
                core_turned[c * tile:(c + 1) * tile, span] = core[span, c * tile:(c + 1) * tile].T
            return 0

        lax.fori_loop(0, virtual // tile, turn, 0)

    def kept_result(slot, pair):
        return pltpu.make_async_copy(
            result.at[slot, own_plane * columns + lax.rem(row + own_first, columns)],
            out_ref.at[pair], kept_sems.at[slot])

    def sent_result(slot):
        part = result.at[slot, pl.ds(0, 2 * columns - 1)]
        pltpu.make_async_copy(part, part, result_send.at[slot]).wait()
        kept_result(slot, 0).wait()

    def give(item_step, slot, t):
        pair = pairs_of(item_step, row, slot, occupied)
        for n in range(per):
            q = t * per + n
            to = lax.rem(q + own_first, columns)
            for p in range(2):
                plane = lax.rem(own_plane + 1 + p, 2)
                where = lax.select(own_plane == plane, z, mate)

                @pl.when((own_plane != plane) | (to != row))
                def _():
                    pltpu.make_async_remote_copy(
                        src_ref=result.at[slot, plane * columns + q], dst_ref=out_ref.at[pair],
                        send_sem=result_send.at[slot], recv_sem=out_sems.at[item_step],
                        device_id=(to, where), device_id_type=MESH,
                    ).start()

    def keep(item_step, slot):
        kept_result(slot, pairs_of(item_step, row, slot, occupied)).start()

    def ladder_item(item):
        alone, step, straight, flipped = item_of(item)
        loads = [
            pltpu.make_async_copy(
                slabs_ref.at[step, :, pl.ds(own_first, rows_in_half)], held.at[own_plane, :, pl.ds(0, rows_in_half)],
                load_sems.at[0]),
            pltpu.make_async_copy(
                slabs_ref.at[step, :, pl.ds(far_first, rows_in_half)],
                held.at[own_plane, :, pl.ds(rows_in_half, rows_in_half)], load_sems.at[1]),
            pltpu.make_async_copy(
                outer_ref.at[step, :, pl.ds(own_first, rows_in_half)],
                held.at[1 - own_plane, :, pl.ds(0, rows_in_half)], load_sems.at[2]),
            pltpu.make_async_copy(
                outer_ref.at[step, :, pl.ds(far_first, rows_in_half)],
                held.at[1 - own_plane, :, pl.ds(rows_in_half, rows_in_half)], load_sems.at[3]),
        ]
        for copy in loads:
            copy.start()

        @pl.when(item < steps)
        def _():
            raw(slabs_ref, step, 0).wait_recv()
            raw(slabs_ref, step, 1).wait_recv()

        received = pltpu.make_async_copy(raw_ref.at[step], other, load_sems.at[4])
        received.start()
        for copy in loads + [received]:
            copy.wait()

        def square_load(span, across_span, sem):
            return pltpu.make_async_copy(
                square_ref.at[item, span, across_span],
                summed.at[pl.ds(half + span.start, span.size), pl.ds(half + across_span.start, across_span.size)],
                load_sems.at[sem])

        def assemble():
            for a in range(2):
                for b in range(2):
                    here = slice(a * tile, (a + 1) * tile)
                    there = slice(half + b * tile, half + (b + 1) * tile)
                    here_rows = slice(a * per, (a + 1) * per)
                    near_rows = slice(b * per, (b + 1) * per)
                    there_rows = slice(rows_in_half + b * per, rows_in_half + (b + 1) * per)

                    def block(ref, plane, slot, which):
                        return ref[plane, slot, which].reshape(tile, cols)

                    summed[here, b * tile:(b + 1) * tile] = (
                        block(held, b, straight, here_rows) + block(held, a, flipped, near_rows).T)
                    summed[here, there] = block(other, b, straight, here_rows) + block(held, a, flipped, there_rows).T
                    summed[there, here] = block(held, a, straight, there_rows) + block(other, b, flipped, here_rows).T

        def first(t, _):
            span = pl.ds(pl.multiple_of(t * tile, tile), tile)
            left[span, :] = jnp.dot(
                summed[span, :].astype(jnp.bfloat16), factors[...], preferred_element_type=jnp.float32
            ).astype(jnp.bfloat16)
            return 0

        assemble()
        lax.fori_loop(0, half // tile, first, 0)

        @pl.when(jnp.logical_not(alone))
        def _():
            square(item).wait_recv()
            load = square_load(everything, everything, 5)
            load.start()
            load.wait()

        @pl.when(alone)
        def _():
            strips_of(item).wait_recv()
            copies = [square_load(span, across_span, 5 + n) for n, (span, across_span) in enumerate(strips)]
            for copy in copies:
                copy.start()
            for copy in copies:
                copy.wait()
            for a in range(1, half // rows):
                for b in range(a):
                    down = slice(half + a * rows, half + (a + 1) * rows)
                    along = slice(half + b * rows, half + (b + 1) * rows)
                    summed[down, along] = summed[along, down].T

        lax.fori_loop(half // tile, virtual // tile, first, 0)

        def second(t, _):
            span = pl.ds(pl.multiple_of(t * tile, tile), tile)
            product = jnp.dot(turned[span, :], left[...], preferred_element_type=jnp.float32)
            weighted[span, :] = (core[span, :] * product).astype(jnp.bfloat16)
            weighted_turned[span, :] = (core_turned[span, :] * product).astype(jnp.bfloat16)
            return 0

        lax.fori_loop(0, virtual // tile, second, 0)

        def third(t, _):
            span = pl.ds(pl.multiple_of(t * tile, tile), tile)
            right[span, :] = jnp.dot(
                weighted[span, :], turned[:, 0:half], preferred_element_type=jnp.float32
            ).astype(jnp.bfloat16)
            return 0

        lax.fori_loop(0, virtual // tile, third, 0)

        @pl.when((item > 0) & (item <= steps - 1))
        def _():
            sent_result(0)

        @pl.when(((item > 0) & (item < steps - 1)) | (item == steps))
        def _():
            sent_result(1)

        def fourth(t, _):
            span = pl.ds(pl.multiple_of(t * tile, tile), tile)
            value = summed[span, 0:half] + jnp.dot(
                factors[span, :], right[...], preferred_element_type=jnp.float32)
            for p in range(2):
                for n in range(per):
                    result[straight, p * columns + t * per + n] = (
                        value[n * rows:(n + 1) * rows, p * tile:(p + 1) * tile])
            give(step, straight, t)
            return 0

        lax.fori_loop(0, virtual // tile, fourth, 0)
        keep(step, straight)

        @pl.when(jnp.logical_not(alone))
        def _():
            for b in range(2):
                right_turned[b * tile:(b + 1) * tile, :] = jnp.dot(
                    factors[b * tile:(b + 1) * tile, :], weighted_turned[...], preferred_element_type=jnp.float32
                ).astype(jnp.bfloat16)

            def fifth(t, _):
                span = pl.ds(pl.multiple_of(t * tile, tile), tile)
                for p in range(2):
                    value = summed[p * tile:(p + 1) * tile, span] + jnp.dot(
                        right_turned[p * tile:(p + 1) * tile, :], turned[:, span],
                        preferred_element_type=jnp.float32)
                    value = value.T
                    for n in range(per):
                        result[1, p * columns + t * per + n] = value[n * rows:(n + 1) * rows, :]
                give(step, 1, t)
                return 0

            lax.fori_loop(0, virtual // tile, fifth, 0)
            keep(step, 1)

    groups = steps // group
    opening()

    @pl.when(jnp.logical_not(inner))
    def _():
        relay(0).wait_send()
        relay(1).start()

        def outer_group(g, _):
            hole_group(g)
            for n in range(group):
                step = g * group + n
                wait_slab(step)
                relay(step - 1).wait_send()
                relay(step).start()
            return 0

        lax.fori_loop(1, groups, outer_group, 0)
        relay(steps - 1).wait_send()

    @pl.when(inner)
    def _():
        pack(0)

        def body(item, _):
            @pl.when((lax.rem(item, group) == 0) & (item < steps - group))
            def _():
                hole_group(item // group + 1)

            @pl.when(item < steps)
            def _():
                pack(item + 1)

            ladder_item(item)

            @pl.when(item + 2 < steps)
            def _():
                raw_own(item + 2)

            return 0

        lax.fori_loop(0, steps + 1, body, 0)

        def finish(n, _):
            raw(slabs_ref, n // 2, lax.rem(n, 2)).wait_send()
            return 0

        lax.fori_loop(0, 2 * steps, finish, 0)
        strips_of(steps - 1).wait_send()
        strips_of(steps).wait_send()
        sent_result(0)
        sent_result(1)

    sent_stage().wait()

    def arrived(tiles_of_step):
        def wait(step, _):
            part = out_ref.at[pl.ds(0, tiles_of_step)]
            pltpu.make_async_copy(part, part, out_sems.at[step]).wait()
            return 0

        lax.fori_loop(0, steps, wait, 0)

    @pl.when(inner)
    def _():
        arrived(2 * (columns - 1))

    @pl.when(jnp.logical_not(inner))
    def _():
        arrived(2 * columns)


def halves(amplitudes, hole_ints, factors, core_matrix, columns):
    occupied, _, rows, cols = amplitudes.shape
    pairs = occupied * occupied
    virtual = factors.shape[0]
    grid_points = factors.shape[1]
    steps = occupied
    half = virtual // 2
    tile = half // 2
    group = 2
    f32, bf16 = jnp.float32, jnp.bfloat16
    hbm = pl.BlockSpec(memory_space=pl.ANY)
    vmem = pl.BlockSpec(memory_space=pltpu.VMEM)
    dma = pltpu.SemaphoreType.DMA
    outs = pl.pallas_call(
        halves_kernel,
        in_specs=[vmem, hbm, hbm, hbm],
        out_specs=[hbm] * 5,
        out_shape=[
            jax.ShapeDtypeStruct((pairs, rows, cols), f32),
            jax.ShapeDtypeStruct((steps, 2, columns, rows, cols), f32),
            jax.ShapeDtypeStruct((steps, 2, columns, rows, cols), f32),
            jax.ShapeDtypeStruct((steps, 2, 2, columns // 2, rows, cols), f32),
            jax.ShapeDtypeStruct((steps + 1, half, half), f32),
        ],
        scratch_shapes=[
            pltpu.VMEM((2, pairs, 8, cols), f32),
            pltpu.VMEM((group * 2 * columns, rows, cols), f32),
            pltpu.VMEM((group * 2 * columns, pairs), f32),
            pltpu.VMEM((virtual, grid_points), bf16),
            pltpu.VMEM((grid_points, virtual), bf16),
            pltpu.VMEM((grid_points, grid_points), f32),
            pltpu.VMEM((grid_points, grid_points), f32),
            pltpu.VMEM((grid_points, grid_points), bf16),
            pltpu.VMEM((grid_points, grid_points), bf16),
            pltpu.VMEM((virtual, grid_points), bf16),
            pltpu.VMEM((virtual, virtual), f32),
            pltpu.VMEM((2, 2, columns, rows, cols), f32),
            pltpu.VMEM((2, 2, columns // 2, rows, cols), f32),
            pltpu.VMEM((grid_points, half), bf16),
            pltpu.VMEM((half, grid_points), bf16),
            pltpu.VMEM((2, 2 * columns, rows, cols), f32),
            pltpu.VMEM((2, 2, columns // 2, rows, cols), f32),
            pltpu.VMEM((2, half, half), f32),
            dma((2,)),
            dma,
            dma((steps,)),
            dma((group, 8)),
            dma((steps,)),
            dma((steps,)),
            dma((2 * steps,)),
            dma((2 * steps,)),
            dma((2,)),
            dma((steps + 1,)),
            dma((2,)),
            dma((2,)),
            dma((steps,)),
            dma((5 + half // rows,)),
        ],
        compiler_params=pltpu.CompilerParams(
            vmem_limit_bytes=VMEM_LIMIT, collective_id=0, has_side_effects=True),
        name="halves",
    )(hole_ints, amplitudes.reshape(pairs, rows, cols), factors, core_matrix)
    return outs[0].reshape(amplitudes.shape)


def local(amplitudes, hole_ints, factors, core_matrix):
    row_count = lax.axis_size("row")
    col_count = lax.axis_size("col")
    devices = row_count * col_count
    occupied, _, rows, cols = amplitudes.shape
    if (row_count, col_count, occupied, rows, cols) == (8, 4, 16, 128, 256):
        return halves(amplitudes, hole_ints, factors, core_matrix, row_count)
    pairs = occupied * occupied
    chunks = pairs // (2 * devices)
    slots = 2 * devices
    flattened = amplitudes.reshape(pairs, rows, cols)
    order = couple_order(occupied)
    weights = jnp.take(hole_ints, jnp.asarray(order), axis=0)
    turned = factors.T
    me = lax.axis_index(("row", "col"))
    first_diagonal = occupied * (occupied - 1) // 2

    arrived = []
    for k in range(chunks):
        term = hole(weights[k * slots:(k + 1) * slots], flattened)
        arrived.append(exchange(term.reshape(devices, 2, rows, cols)))
    returned = []
    for k in range(chunks):
        blocks = arrived[k].reshape(row_count, col_count, 2, rows, cols)
        diagonal = (k * devices + me >= first_diagonal).astype(jnp.int32).reshape(1)
        result = ladder(diagonal, blocks, factors, turned, core_matrix)
        returned.append(exchange(result.reshape(devices, 2, rows, cols)))
    residual = None
    for k in range(chunks):
        residual = place(
            returned[k].reshape(slots, rows, cols), residual, order[k * slots:(k + 1) * slots], pairs
        )
    return residual.reshape(amplitudes.shape)


def solution(mesh):
    return jax.shard_map(
        local,
        mesh=mesh,
        in_specs=(P(None, None, "row", "col"), P(), P(), P()),
        out_specs=P(None, None, "row", "col"),
        check_vma=False,
    )
```

```python
import functools

import jax
import jax.numpy as jnp
import numpy as np
from jax import lax
from jax.experimental import pallas as pl
from jax.experimental.pallas import tpu as pltpu
from jax.sharding import PartitionSpec as P

VMEM_LIMIT = 60 * 1024 * 1024


def couple_order(occupied):
    listing = []
    for first in range(occupied):
        for second in range(first + 1, occupied):
            listing += [first * occupied + second, second * occupied + first]
    listing += [first * occupied + first for first in range(occupied)]
    return np.array(listing, dtype=np.int32)


def hole_kernel(weights_ref, amplitudes_ref, out_ref):
    weights = weights_ref[...]
    slots = weights.shape[0]
    high = weights.astype(jnp.bfloat16)
    low = (weights - high.astype(jnp.float32)).astype(jnp.bfloat16)
    both = jnp.concatenate([high, low], axis=0)
    by_row = jnp.swapaxes(amplitudes_ref[...], 0, 1)
    terms = []
    for row in range(by_row.shape[0]):
        values = by_row[row]
        top = values.astype(jnp.bfloat16)
        rest = (values - top.astype(jnp.float32)).astype(jnp.bfloat16)
        main = jnp.dot(both, top, preferred_element_type=jnp.float32)
        small = jnp.dot(high, rest, preferred_element_type=jnp.float32)
        terms.append(main[:slots] + (main[slots:] + small))
    out_ref[...] = jnp.swapaxes(jnp.stack(terms, axis=0), 0, 1)


def hole(weights, amplitudes):
    slots, pairs = weights.shape
    _, rows, cols = amplitudes.shape
    step = 8
    return pl.pallas_call(
        hole_kernel,
        grid=(rows // step,),
        in_specs=[
            pl.BlockSpec((slots, pairs), lambda i: (0, 0)),
            pl.BlockSpec((pairs, step, cols), lambda i: (0, i, 0)),
        ],
        out_specs=pl.BlockSpec((slots, step, cols), lambda i: (0, i, 0)),
        out_shape=jax.ShapeDtypeStruct((slots, rows, cols), jnp.float32),
        compiler_params=pltpu.CompilerParams(vmem_limit_bytes=VMEM_LIMIT),
        cost_estimate=pl.CostEstimate(
            flops=6 * slots * pairs * rows * cols,
            bytes_accessed=4 * (slots + pairs) * rows * cols,
            transcendentals=0,
        ),
        name="hole",
    )(weights, amplitudes)


def ladder_kernel(diagonal_ref, blocks_ref, factors_ref, turned_ref, core_ref, out_ref,
                  summed, left, weighted):
    row_count, col_count, _, rows, cols = blocks_ref.shape
    virtual = row_count * rows
    grid_points = factors_ref.shape[1]
    tile = 256
    row_blocks = tile // rows
    col_blocks = tile // cols
    tiles = virtual // tile

    def one(which, _):
        partner = jnp.where(diagonal_ref[0] != 0, which, 1 - which)

        def first(t, _):
            span = pl.ds(pl.multiple_of(t * tile, tile), tile)
            for c in range(tiles):
                straight = jnp.concatenate(
                    [
                        jnp.concatenate(
                            [blocks_ref[t * row_blocks + r, c * col_blocks + q, which] for q in range(col_blocks)],
                            axis=1,
                        )
                        for r in range(row_blocks)
                    ],
                    axis=0,
                )
                other = jnp.concatenate(
                    [
                        jnp.concatenate(
                            [blocks_ref[c * row_blocks + r, t * col_blocks + q, partner] for q in range(col_blocks)],
                            axis=1,
                        )
                        for r in range(row_blocks)
                    ],
                    axis=0,
                )
                summed[span, c * tile:(c + 1) * tile] = straight + other.T
            left[span, :] = jnp.dot(
                summed[span, :].astype(jnp.bfloat16), factors_ref[...], preferred_element_type=jnp.float32
            ).astype(jnp.bfloat16)
            return 0

        lax.fori_loop(0, tiles, first, 0)

        def second(t, _):
            span = pl.ds(pl.multiple_of(t * tile, tile), tile)
            inner = jnp.dot(turned_ref[span, :], left[...], preferred_element_type=jnp.float32)
            weighted[span, :] = (core_ref[span, :] * inner).astype(jnp.bfloat16)
            return 0

        lax.fori_loop(0, grid_points // tile, second, 0)

        def third(t, _):
            span = pl.ds(pl.multiple_of(t * tile, tile), tile)
            spread = jnp.dot(
                factors_ref[span, :], weighted[...], preferred_element_type=jnp.float32
            ).astype(jnp.bfloat16)
            result = summed[span, :] + jnp.dot(spread, turned_ref[...], preferred_element_type=jnp.float32)
            for r in range(row_blocks):
                for c in range(col_count):
                    out_ref[t * row_blocks + r, c, which] = result[r * rows:(r + 1) * rows, c * cols:(c + 1) * cols]
            return 0

        lax.fori_loop(0, tiles, third, 0)
        return 0

    lax.fori_loop(0, 2, one, 0)


def ladder(diagonal, blocks, factors, turned, core_matrix):
    row_count, _, _, rows, _ = blocks.shape
    virtual = row_count * rows
    grid_points = factors.shape[1]
    vmem = pl.BlockSpec(memory_space=pltpu.VMEM)
    return pl.pallas_call(
        ladder_kernel,
        in_specs=[pl.BlockSpec(memory_space=pltpu.SMEM), vmem, vmem, vmem, vmem],
        out_specs=vmem,
        out_shape=jax.ShapeDtypeStruct(blocks.shape, jnp.float32),
        scratch_shapes=[
            pltpu.VMEM((virtual, virtual), jnp.float32),
            pltpu.VMEM((virtual, grid_points), jnp.bfloat16),
            pltpu.VMEM((grid_points, grid_points), jnp.bfloat16),
        ],
        compiler_params=pltpu.CompilerParams(vmem_limit_bytes=VMEM_LIMIT),
        cost_estimate=pl.CostEstimate(
            flops=16 * virtual * virtual * grid_points,
            bytes_accessed=24 * virtual * virtual,
            transcendentals=0,
        ),
        name="ladder",
    )(diagonal, blocks, factors, turned, core_matrix)


def place_kernel(places, group, blocks_ref, *refs):
    out_ref, held, in_sems, out_sems = refs[-4:]
    slots = len(places)

    def fetch(g):
        span = pl.ds(g * group, group)
        return pltpu.make_async_copy(blocks_ref.at[span], held.at[span], in_sems.at[g])

    def put(s):
        return pltpu.make_async_copy(held.at[s], out_ref.at[places[s]], out_sems.at[s])

    for g in range(slots // group):
        fetch(g).start()
    for g in range(slots // group):
        fetch(g).wait()
        for s in range(g * group, (g + 1) * group):
            put(s).start()
    for s in range(slots):
        put(s).wait()


def place(blocks, target, places, pairs):
    slots, rows, cols = blocks.shape
    group = max(1, slots // 8)
    hbm = pl.BlockSpec(memory_space=pl.ANY)
    operands = (blocks,) if target is None else (blocks, target)
    return pl.pallas_call(
        functools.partial(place_kernel, [int(p) for p in places], group),
        in_specs=[hbm] * len(operands),
        out_specs=hbm,
        out_shape=jax.ShapeDtypeStruct((pairs, rows, cols), jnp.float32),
        scratch_shapes=[
            pltpu.VMEM((slots, rows, cols), jnp.float32),
            pltpu.SemaphoreType.DMA((slots // group,)),
            pltpu.SemaphoreType.DMA((slots,)),
        ],
        input_output_aliases={} if target is None else {1: 0},
        compiler_params=pltpu.CompilerParams(vmem_limit_bytes=VMEM_LIMIT),
        cost_estimate=pl.CostEstimate(flops=0, bytes_accessed=8 * slots * rows * cols, transcendentals=0),
        name="place",
    )(*operands)


def exchange(blocks):
    return lax.all_to_all(blocks, ("row", "col"), split_axis=0, concat_axis=0, tiled=True)


MESH = pl.DeviceIdType.MESH


def pairs_of(step, column, slot, occupied):
    odd = occupied - 1
    first = lax.select(column == 0, jnp.int32(odd), lax.rem(step + column, odd))
    second = lax.select(column == 0, step, lax.rem(step + odd - column, odd))
    straight = lax.select(slot == 0, first * occupied + second, second * occupied + first)
    alone = (slot * (occupied // 2) + column) * (occupied + 1)
    return lax.select(step == odd, alone, straight)


def halves_kernel(weights_ref, amplitudes_ref, factors_hbm, core_hbm,
                  out_ref, slabs_ref, outer_ref, raw_ref, square_ref,
                  tiles, stage, chosen, factors, turned, core, core_turned, weighted, weighted_turned,
                  left, known, summed, held, other, right, right_turned, result, packing, squares,
                  tile_sems, stage_sem, slab_sems, open_sems, relay_send, relay_recv, raw_send, raw_recv,
                  square_send, square_recv, result_send, kept_sems, out_sems, load_sems):
    row = lax.axis_index("row")
    z = lax.axis_index("col")
    pairs, rows, cols = amplitudes_ref.shape
    steps, _, columns, _, _ = slabs_ref.shape
    occupied = steps
    virtual = columns * rows
    half = virtual // 2
    tile = half // 2
    per = tile // rows
    upper = z // 2
    inner = (z == 1) | (z == 2)
    mate = z + 1 - 2 * lax.rem(z, 2)
    across = 3 - z
    own_plane = 1 - upper
    own_rows = pl.multiple_of(upper * half, half)
    far_rows = pl.multiple_of(half - upper * half, half)
    rows_in_half = columns // 2
    own_first = upper * rows_in_half
    far_first = rows_in_half - own_first
    group = stage.shape[0] // (2 * columns)
    chunks = open_sems.shape[1]
    chunk_rows = rows // chunks
    blocks = rows // 8

    barrier = pltpu.get_barrier_semaphore()
    for d in range(1, columns):
        pl.semaphore_signal(barrier, 1, device_id=(lax.rem(row + d, columns), z), device_id_type=MESH)
    for d in range(columns):
        pl.semaphore_signal(barrier, 1, device_id=(d, mate), device_id_type=MESH)

    @pl.when(inner)
    def _():
        pl.semaphore_signal(barrier, 1, device_id=(row, across), device_id_type=MESH)

    def fetch(b, slot):
        return pltpu.make_async_copy(
            amplitudes_ref.at[:, pl.ds(pl.multiple_of(b * 8, 8), 8), :], tiles.at[slot], tile_sems.at[slot]
        )

    def sent_stage():
        part = stage.at[pl.ds(0, 2 * group * (columns - 1))]
        return pltpu.make_async_copy(part, part, stage_sem)

    def choose(g):
        fetch(0, 0).start()

        def take(n, _):
            step = g * group + n // (2 * columns)
            pair = pairs_of(step, lax.rem(n // 2, columns), lax.rem(n, 2), occupied)
            chosen[pl.ds(n, 1), :] = weights_ref[pl.ds(pair, 1), :]
            return 0

        lax.fori_loop(0, chosen.shape[0], take, 0)

    def hole_rows(start, count):
        weights = chosen[...]
        slots = weights.shape[0]
        high = weights.astype(jnp.bfloat16)
        low = (weights - high.astype(jnp.float32)).astype(jnp.bfloat16)
        both = jnp.concatenate([high, low], axis=0)

        def block(n, _):
            b = start + n
            slot = lax.rem(b, 2)

            @pl.when(b + 1 < blocks)
            def _():
                fetch(b + 1, 1 - slot).start()

            fetch(b, slot).wait()
            by_row = jnp.swapaxes(tiles[slot], 0, 1)
            terms = []
            for m in range(8):
                values = by_row[m]
                top = values.astype(jnp.bfloat16)
                rest = (values - top.astype(jnp.float32)).astype(jnp.bfloat16)
                main = jnp.dot(both, top, preferred_element_type=jnp.float32)
                small = jnp.dot(high, rest, preferred_element_type=jnp.float32)
                terms.append(main[:slots] + (main[slots:] + small))
            stage[:, pl.ds(pl.multiple_of(b * 8, 8), 8), :] = jnp.swapaxes(jnp.stack(terms, axis=0), 0, 1)
            return 0

        lax.fori_loop(0, count, block, 0)

    def send_tiles(n, step, span, arrival):
        for d in range(1, columns):
            to = lax.rem(row + d, columns)
            pltpu.make_async_remote_copy(
                src_ref=stage.at[pl.ds((n * columns + to) * 2, 2), span, :],
                dst_ref=slabs_ref.at[step, :, row, span, :],
                send_sem=stage_sem,
                recv_sem=arrival,
                device_id=(to, z),
                device_id_type=MESH,
            ).start()
        pltpu.make_async_copy(
            stage.at[pl.ds((n * columns + row) * 2, 2), span, :], slabs_ref.at[step, :, row, span, :], arrival
        ).start()

    def hole_group(g):
        choose(g)
        sent_stage().wait()
        hole_rows(0, blocks)

        def send(n, _):
            step = g * group + n
            send_tiles(n, step, pl.ds(0, rows), slab_sems.at[step])
            return 0

        lax.fori_loop(0, group, send, 0)

    def chunk_of(c):
        return pl.ds(pl.multiple_of(c * chunk_rows, chunk_rows), chunk_rows)

    def forward_chunk(step, c):
        span = chunk_of(c)
        part = slabs_ref.at[step, :, :, span, :]
        pltpu.make_async_copy(part, part, open_sems.at[step, c]).wait()

        @pl.when(inner)
        def _():
            pltpu.make_async_remote_copy(
                src_ref=slabs_ref.at[step, :, pl.ds(far_first, rows_in_half), span, :],
                dst_ref=raw_ref.at[step, own_plane, :, :, span, :],
                send_sem=raw_send.at[2 * step + own_plane], recv_sem=raw_recv.at[2 * step + own_plane],
                device_id=(row, across), device_id_type=MESH,
            ).start()

        @pl.when(jnp.logical_not(inner) & (step == 0))
        def _():
            pltpu.make_async_remote_copy(
                src_ref=part, dst_ref=outer_ref.at[step, :, :, span, :],
                send_sem=relay_send.at[step], recv_sem=relay_recv.at[step],
                device_id=(row, mate), device_id_type=MESH,
            ).start()

    def opening():
        window = 6
        choose(0)
        hole_rows(0, blocks // chunks)

        @pl.when(inner)
        def _():
            pl.semaphore_wait(barrier, 2 * columns)

        @pl.when(jnp.logical_not(inner))
        def _():
            pl.semaphore_wait(barrier, 2 * columns - 1)

        def chunk(c, _):
            send_tiles(0, 0, chunk_of(c), open_sems.at[0, c])

            @pl.when(c >= window)
            def _():
                forward_chunk(0, c - window)

            @pl.when(c + 1 < chunks)
            def _():
                hole_rows((c + 1) * (blocks // chunks), blocks // chunks)

            return 0

        lax.fori_loop(0, chunks, chunk, 0)

        def follow(c, _):
            step = lax.select(c < window, jnp.int32(0), jnp.int32(1))
            forward_chunk(step, lax.rem(c + chunks - window, chunks))
            send_tiles(1, 1, chunk_of(c), open_sems.at[1, c])
            return 0

        lax.fori_loop(0, chunks, follow, 0)

        @pl.when(inner)
        def _():
            prepare()

        for c in range(chunks - window, chunks):
            forward_chunk(1, c)

    def wait_slab(step):
        pltpu.make_async_copy(slabs_ref.at[step], slabs_ref.at[step], slab_sems.at[step]).wait()

    def relay(step):
        return pltpu.make_async_remote_copy(
            src_ref=slabs_ref.at[step], dst_ref=outer_ref.at[step],
            send_sem=relay_send.at[step], recv_sem=relay_recv.at[step],
            device_id=(row, mate), device_id_type=MESH,
        )

    def raw(source, step, plane):
        return pltpu.make_async_remote_copy(
            src_ref=source.at[step, :, pl.ds(far_first, rows_in_half)], dst_ref=raw_ref.at[step, plane],
            send_sem=raw_send.at[2 * step + plane], recv_sem=raw_recv.at[2 * step + plane],
            device_id=(row, across), device_id_type=MESH,
        )

    def square_copy(item, span, across_span):
        slot = lax.rem(item, 2)
        return pltpu.make_async_remote_copy(
            src_ref=squares.at[slot, span, across_span], dst_ref=square_ref.at[item, span, across_span],
            send_sem=square_send.at[slot], recv_sem=square_recv.at[item],
            device_id=(row, across), device_id_type=MESH,
        )

    strips = [(pl.ds(s * rows, rows), pl.ds(s * rows, half - s * rows)) for s in range(half // rows)]
    everything = pl.ds(0, half)
    strip_bytes_rows = sum((half - s * rows) * rows for s in range(half // rows)) // half

    def square(item):
        return square_copy(item, everything, everything)

    def strips_of(item):
        return square_copy(item, pl.ds(0, strip_bytes_rows), everything)

    def item_of(item):
        alone = item >= steps - 1
        step = jnp.minimum(item, steps - 1)
        straight = lax.select(alone, item - (steps - 1), jnp.int32(0))
        flipped = lax.select(alone, item - (steps - 1), jnp.int32(1))
        return alone, step, straight, flipped

    def raw_own(step):
        wait_slab(step)
        raw(slabs_ref, step, own_plane).start()

    def pack(item):
        alone, step, straight, flipped = item_of(item)

        @pl.when(item < steps)
        def _():
            relay(step).wait_recv()
            raw(outer_ref, step, 1 - own_plane).start()

        mine = pltpu.make_async_copy(
            slabs_ref.at[step, :, pl.ds(own_first, rows_in_half)], packing.at[own_plane], load_sems.at[0])
        theirs = pltpu.make_async_copy(
            outer_ref.at[step, :, pl.ds(own_first, rows_in_half)], packing.at[1 - own_plane], load_sems.at[1])
        mine.start()
        theirs.start()

        @pl.when(item >= 2)
        def _():
            square(item).wait_send()

        mine.wait()
        theirs.wait()
        slot = lax.rem(item, 2)
        for a in range(2):
            for b in range(2):
                squares[slot, a * tile:(a + 1) * tile, b * tile:(b + 1) * tile] = (
                    packing[b, straight, a * per:(a + 1) * per].reshape(tile, cols)
                    + packing[a, flipped, b * per:(b + 1) * per].reshape(tile, cols).T
                )

        @pl.when(jnp.logical_not(alone))
        def _():
            square(item).start()

        @pl.when(alone)
        def _():
            for span, across_span in strips:
                square_copy(item, span, across_span).start()

    def prepare():
        top = pltpu.make_async_copy(
            factors_hbm.at[pl.ds(own_rows, half), :], factors.at[pl.ds(0, half), :], load_sems.at[0])
        bottom = pltpu.make_async_copy(
            factors_hbm.at[pl.ds(far_rows, half), :], factors.at[pl.ds(half, half), :], load_sems.at[1])
        whole = pltpu.make_async_copy(core_hbm, core, load_sems.at[2])
        for copy in (top, bottom, whole):
            copy.start()
        for copy in (top, bottom, whole):
            copy.wait()

        def turn(t, _):
            span = pl.ds(pl.multiple_of(t * tile, tile), tile)
            for c in range(virtual // tile):
                turned[c * tile:(c + 1) * tile, span] = factors[span, c * tile:(c + 1) * tile].T
                core_turned[c * tile:(c + 1) * tile, span] = core[span, c * tile:(c + 1) * tile].T
            return 0

        lax.fori_loop(0, virtual // tile, turn, 0)

    def kept_result(slot, pair):
        return pltpu.make_async_copy(
            result.at[slot, own_plane * columns + lax.rem(row + own_first, columns)],
            out_ref.at[pair], kept_sems.at[slot])

    def sent_result(slot):
        part = result.at[slot, pl.ds(0, 2 * columns - 1)]
        pltpu.make_async_copy(part, part, result_send.at[slot]).wait()
        kept_result(slot, 0).wait()

    def give(item_step, slot, t, plane):
        pair = pairs_of(item_step, row, slot, occupied)
        for n in range(per):
            q = t * per + n
            to = lax.rem(q + own_first, columns)
            where = lax.select(own_plane == plane, z, mate)

            @pl.when((own_plane != plane) | (to != row))
            def _():
                pltpu.make_async_remote_copy(
                    src_ref=result.at[slot, plane * columns + q], dst_ref=out_ref.at[pair],
                    send_sem=result_send.at[slot], recv_sem=out_sems.at[item_step],
                    device_id=(to, where), device_id_type=MESH,
                ).start()

    def keep(item_step, slot):
        kept_result(slot, pairs_of(item_step, row, slot, occupied)).start()

    def ladder_item(item):
        alone, step, straight, flipped = item_of(item)
        loads = [
            pltpu.make_async_copy(
                slabs_ref.at[step, :, pl.ds(own_first, rows_in_half)], held.at[own_plane, :, pl.ds(0, rows_in_half)],
                load_sems.at[0]),
            pltpu.make_async_copy(
                slabs_ref.at[step, :, pl.ds(far_first, rows_in_half)],
                held.at[own_plane, :, pl.ds(rows_in_half, rows_in_half)], load_sems.at[1]),
            pltpu.make_async_copy(
                outer_ref.at[step, :, pl.ds(own_first, rows_in_half)],
                held.at[1 - own_plane, :, pl.ds(0, rows_in_half)], load_sems.at[2]),
            pltpu.make_async_copy(
                outer_ref.at[step, :, pl.ds(far_first, rows_in_half)],
                held.at[1 - own_plane, :, pl.ds(rows_in_half, rows_in_half)], load_sems.at[3]),
        ]
        for copy in loads:
            copy.start()

        @pl.when(item < steps)
        def _():
            raw(slabs_ref, step, 0).wait_recv()
            raw(slabs_ref, step, 1).wait_recv()

        received = pltpu.make_async_copy(raw_ref.at[step], other, load_sems.at[4])
        received.start()
        for copy in loads + [received]:
            copy.wait()

        def square_load(span, across_span, sem):
            return pltpu.make_async_copy(
                square_ref.at[item, span, across_span],
                summed.at[pl.ds(half + span.start, span.size), pl.ds(half + across_span.start, across_span.size)],
                load_sems.at[sem])

        def assemble():
            for a in range(2):
                for b in range(2):
                    here = slice(a * tile, (a + 1) * tile)
                    there = slice(half + b * tile, half + (b + 1) * tile)
                    here_rows = slice(a * per, (a + 1) * per)
                    near_rows = slice(b * per, (b + 1) * per)
                    there_rows = slice(rows_in_half + b * per, rows_in_half + (b + 1) * per)

                    def block(ref, plane, slot, which):
                        return ref[plane, slot, which].reshape(tile, cols)

                    summed[here, b * tile:(b + 1) * tile] = (
                        block(held, b, straight, here_rows) + block(held, a, flipped, near_rows).T)
                    summed[here, there] = block(other, b, straight, here_rows) + block(held, a, flipped, there_rows).T
                    summed[there, here] = block(held, a, straight, there_rows) + block(other, b, flipped, here_rows).T

        def product_known(t, _):
            span = pl.ds(pl.multiple_of(t * tile, tile), tile)
            known[span, :] = jnp.dot(turned[span, :], left[...], preferred_element_type=jnp.float32)
            return 0

        def first(t, _):
            span = pl.ds(pl.multiple_of(t * tile, tile), tile)
            left[span, :] = jnp.dot(
                summed[span, :].astype(jnp.bfloat16), factors[...], preferred_element_type=jnp.float32
            ).astype(jnp.bfloat16)
            return 0

        def part_of_first(t, begin):
            span = pl.ds(pl.multiple_of(t * tile, tile), tile)
            left[span, :] = jnp.dot(
                summed[span, begin:begin + half].astype(jnp.bfloat16), factors[begin:begin + half, :],
                preferred_element_type=jnp.float32,
            ).astype(jnp.bfloat16)
            return 0

        assemble()
        lax.fori_loop(0, half // tile, first, 0)
        lax.fori_loop(half // tile, virtual // tile, lambda t, _: part_of_first(t, 0), 0)
        lax.fori_loop(0, virtual // tile, product_known, 0)

        @pl.when(jnp.logical_not(alone))
        def _():
            square(item).wait_recv()
            load = square_load(everything, everything, 5)
            load.start()
            load.wait()

        @pl.when(alone)
        def _():
            strips_of(item).wait_recv()
            copies = [square_load(span, across_span, 5 + n) for n, (span, across_span) in enumerate(strips)]
            for copy in copies:
                copy.start()
            for copy in copies:
                copy.wait()
            for a in range(1, half // rows):
                for b in range(a):
                    down = slice(half + a * rows, half + (a + 1) * rows)
                    along = slice(half + b * rows, half + (b + 1) * rows)
                    summed[down, along] = summed[along, down].T

        lax.fori_loop(half // tile, virtual // tile, lambda t, _: part_of_first(t, half), 0)

        def second(t, _):
            span = pl.ds(pl.multiple_of(t * tile, tile), tile)
            product = known[span, :] + jnp.dot(
                turned[span, half:], left[half:, :], preferred_element_type=jnp.float32)
            weighted[span, :] = (core[span, :] * product).astype(jnp.bfloat16)
            weighted_turned[span, :] = (core_turned[span, :] * product).astype(jnp.bfloat16)
            return 0

        lax.fori_loop(0, virtual // tile, second, 0)

        @pl.when((item > 0) & (item <= steps - 1))
        def _():
            sent_result(0)

        @pl.when(((item > 0) & (item < steps - 1)) | (item == steps))
        def _():
            sent_result(1)

        def plane_columns(m, _):
            plane = lax.rem(own_plane + 1 + m, 2)
            there = pl.ds(pl.multiple_of(plane * tile, tile), tile)

            def third(t, _):
                span = pl.ds(pl.multiple_of(t * tile, tile), tile)
                right[span, :] = jnp.dot(
                    weighted[span, :], turned[:, there], preferred_element_type=jnp.float32
                ).astype(jnp.bfloat16)
                return 0

            lax.fori_loop(0, virtual // tile, third, 0)

            def fourth(t, _):
                span = pl.ds(pl.multiple_of(t * tile, tile), tile)
                value = summed[span, there] + jnp.dot(
                    factors[span, :], right[...], preferred_element_type=jnp.float32)
                for n in range(per):
                    result[straight, plane * columns + t * per + n] = value[n * rows:(n + 1) * rows, :]
                give(step, straight, t, plane)
                return 0

            lax.fori_loop(0, virtual // tile, fourth, 0)
            return 0

        lax.fori_loop(0, 2, plane_columns, 0)
        keep(step, straight)

        @pl.when(jnp.logical_not(alone))
        def _():
            for b in range(2):
                right_turned[b * tile:(b + 1) * tile, :] = jnp.dot(
                    factors[b * tile:(b + 1) * tile, :], weighted_turned[...], preferred_element_type=jnp.float32
                ).astype(jnp.bfloat16)

            def fifth(t, _):
                span = pl.ds(pl.multiple_of(t * tile, tile), tile)
                for p in range(2):
                    value = summed[p * tile:(p + 1) * tile, span] + jnp.dot(
                        right_turned[p * tile:(p + 1) * tile, :], turned[:, span],
                        preferred_element_type=jnp.float32)
                    value = value.T
                    for n in range(per):
                        result[1, p * columns + t * per + n] = value[n * rows:(n + 1) * rows, :]
                give(step, 1, t, 1 - own_plane)
                give(step, 1, t, own_plane)
                return 0

            lax.fori_loop(0, virtual // tile, fifth, 0)
            keep(step, 1)

    groups = steps // group
    opening()

    @pl.when(jnp.logical_not(inner))
    def _():
        relay(0).wait_send()
        relay(1).start()

        def outer_group(g, _):
            hole_group(g)
            for n in range(group):
                step = g * group + n
                wait_slab(step)
                relay(step - 1).wait_send()
                relay(step).start()
            return 0

        lax.fori_loop(1, groups, outer_group, 0)
        relay(steps - 1).wait_send()

    @pl.when(inner)
    def _():
        pack(0)

        def body(item, _):
            @pl.when((lax.rem(item, group) == 0) & (item < steps - group))
            def _():
                hole_group(item // group + 1)

            @pl.when(item < steps)
            def _():
                pack(item + 1)

            ladder_item(item)

            @pl.when(item + 2 < steps)
            def _():
                raw_own(item + 2)

            return 0

        lax.fori_loop(0, steps + 1, body, 0)

        def finish(n, _):
            raw(slabs_ref, n // 2, lax.rem(n, 2)).wait_send()
            return 0

        lax.fori_loop(0, 2 * steps, finish, 0)
        strips_of(steps - 1).wait_send()
        strips_of(steps).wait_send()
        sent_result(0)
        sent_result(1)

    sent_stage().wait()

    def arrived(tiles_of_step):
        def wait(step, _):
            part = out_ref.at[pl.ds(0, tiles_of_step)]
            pltpu.make_async_copy(part, part, out_sems.at[step]).wait()
            return 0

        lax.fori_loop(0, steps, wait, 0)

    @pl.when(inner)
    def _():
        arrived(2 * (columns - 1))

    @pl.when(jnp.logical_not(inner))
    def _():
        arrived(2 * columns)


def halves(amplitudes, hole_ints, factors, core_matrix, columns):
    occupied, _, rows, cols = amplitudes.shape
    pairs = occupied * occupied
    virtual = factors.shape[0]
    grid_points = factors.shape[1]
    steps = occupied
    half = virtual // 2
    tile = half // 2
    group = 2
    f32, bf16 = jnp.float32, jnp.bfloat16
    hbm = pl.BlockSpec(memory_space=pl.ANY)
    vmem = pl.BlockSpec(memory_space=pltpu.VMEM)
    dma = pltpu.SemaphoreType.DMA
    outs = pl.pallas_call(
        halves_kernel,
        in_specs=[vmem, hbm, hbm, hbm],
        out_specs=[hbm] * 5,
        out_shape=[
            jax.ShapeDtypeStruct((pairs, rows, cols), f32),
            jax.ShapeDtypeStruct((steps, 2, columns, rows, cols), f32),
            jax.ShapeDtypeStruct((steps, 2, columns, rows, cols), f32),
            jax.ShapeDtypeStruct((steps, 2, 2, columns // 2, rows, cols), f32),
            jax.ShapeDtypeStruct((steps + 1, half, half), f32),
        ],
        scratch_shapes=[
            pltpu.VMEM((2, pairs, 8, cols), f32),
            pltpu.VMEM((group * 2 * columns, rows, cols), f32),
            pltpu.VMEM((group * 2 * columns, pairs), f32),
            pltpu.VMEM((virtual, grid_points), bf16),
            pltpu.VMEM((grid_points, virtual), bf16),
            pltpu.VMEM((grid_points, grid_points), f32),
            pltpu.VMEM((grid_points, grid_points), f32),
            pltpu.VMEM((grid_points, grid_points), bf16),
            pltpu.VMEM((grid_points, grid_points), bf16),
            pltpu.VMEM((virtual, grid_points), bf16),
            pltpu.VMEM((grid_points, grid_points), f32),
            pltpu.VMEM((virtual, virtual), f32),
            pltpu.VMEM((2, 2, columns, rows, cols), f32),
            pltpu.VMEM((2, 2, columns // 2, rows, cols), f32),
            pltpu.VMEM((grid_points, tile), bf16),
            pltpu.VMEM((half, grid_points), bf16),
            pltpu.VMEM((2, 2 * columns, rows, cols), f32),
            pltpu.VMEM((2, 2, columns // 2, rows, cols), f32),
            pltpu.VMEM((2, half, half), f32),
            dma((2,)),
            dma,
            dma((steps,)),
            dma((group, 16)),
            dma((steps,)),
            dma((steps,)),
            dma((2 * steps,)),
            dma((2 * steps,)),
            dma((2,)),
            dma((steps + 1,)),
            dma((2,)),
            dma((2,)),
            dma((steps,)),
            dma((5 + half // rows,)),
        ],
        compiler_params=pltpu.CompilerParams(
            vmem_limit_bytes=VMEM_LIMIT, collective_id=0, has_side_effects=True),
        name="halves",
    )(hole_ints, amplitudes.reshape(pairs, rows, cols), factors, core_matrix)
    return outs[0].reshape(amplitudes.shape)


def local(amplitudes, hole_ints, factors, core_matrix):
    row_count = lax.axis_size("row")
    col_count = lax.axis_size("col")
    devices = row_count * col_count
    occupied, _, rows, cols = amplitudes.shape
    if (row_count, col_count, occupied, rows, cols) == (8, 4, 16, 128, 256):
        return halves(amplitudes, hole_ints, factors, core_matrix, row_count)
    pairs = occupied * occupied
    chunks = pairs // (2 * devices)
    slots = 2 * devices
    flattened = amplitudes.reshape(pairs, rows, cols)
    order = couple_order(occupied)
    weights = jnp.take(hole_ints, jnp.asarray(order), axis=0)
    turned = factors.T
    me = lax.axis_index(("row", "col"))
    first_diagonal = occupied * (occupied - 1) // 2

    arrived = []
    for k in range(chunks):
        term = hole(weights[k * slots:(k + 1) * slots], flattened)
        arrived.append(exchange(term.reshape(devices, 2, rows, cols)))
    returned = []
    for k in range(chunks):
        blocks = arrived[k].reshape(row_count, col_count, 2, rows, cols)
        diagonal = (k * devices + me >= first_diagonal).astype(jnp.int32).reshape(1)
        result = ladder(diagonal, blocks, factors, turned, core_matrix)
        returned.append(exchange(result.reshape(devices, 2, rows, cols)))
    residual = None
    for k in range(chunks):
        residual = place(
            returned[k].reshape(slots, rows, cols), residual, order[k * slots:(k + 1) * slots], pairs
        )
    return residual.reshape(amplitudes.shape)


def solution(mesh):
    return jax.shard_map(
        local,
        mesh=mesh,
        in_specs=(P(None, None, "row", "col"), P(), P(), P()),
        out_specs=P(None, None, "row", "col"),
        check_vma=False,
    )
```
